256 devices in a mesh: band: 64 (over z, y, core), lev: 4 (over x).
Axes of the slice: x: 4, y: 4, z: 8, core: 2. Of those that a mesh axis runs over, the one named last changes fastest.
Arguments:
- grid_adjoint: float32 [1024, 64, 2048], P('band', 'lev'), may hold values from -6 to 6
- trajectory: float32 [1024, 64, 2048], P('band', 'lev'), may hold values from -3 to 3
- legendre_north: float32 [512, 512, 512], P(('band', 'lev')), may hold values from -0.25 to 0.25
- slot_wavenumber: int32 [512], replicated, may hold values from 0 to 511, each once
- spectral_state: float32 [512, 512, 2, 64], P(('band', 'lev')), may hold values from -6 to 6
- to_modes: float32 [64, 64], replicated, may hold values from -0.75 to 0.75
- from_modes: float32 [64, 64], replicated, may hold values from -0.75 to 0.75
- rates: float32 [64], replicated, may hold values from 0.1 to 10
Outputs:
- spectral_out: float32 [512, 512, 2, 64], P(('band', 'lev'))
- grid_out: float32 [1024, 64, 2048], P('band', 'lev')
The draws below stay inside these ranges and needn't reach their ends.
Inputs may be any that keep to these rules, and one draw needn't show every extreme that they name: `slot_wavenumber`: each wavenumber stands in exactly one slot.
All inputs are finite; a program needn't handle non-finite values.
Results may differ from the reference program's by a relative error of at most 0.000067.
Values sent between devices are 32-bit elements; how exact they have to be, the bound alone decides.
No kernel may reach another device: no remote copies, remote signals or barrier semaphores. Data moves between devices by JAX's collectives and lax.ppermute only.
A program may use at most 128 MiB of HBM per device.

```python
import math
import jax
import jax.numpy as jnp
from jax import lax

M = 512
LAT = 1024
LON = 2048
L = 64
LH = 512


def level_of(key, dims, shards, low, largest):
    factor_of = 1.0
    for axis_at, blocks in shards:
        draws = jax.random.uniform(jax.random.fold_in(jax.random.fold_in(key, 6), axis_at), (blocks,), jnp.float32, low / len(shards), largest / len(shards))
        factor_of = factor_of * jnp.repeat(jnp.exp(draws), dims[axis_at] // blocks).reshape((-1,) + (1,) * (len(dims) - 1 - axis_at))
    return factor_of


def scatter_about(rng, dims, deviation, reach, split=(), kind=jnp.bfloat16):
    entries = jax.random.normal(rng, dims, jnp.float32) * deviation
    if len(split) > 0:
        entries = level_of(rng, dims, split, -0.22, 0.18) * entries
    return jnp.clip(entries, min=-reach, max=reach).astype(kind)


def setup_inputs(seed: int = 0) -> dict:
    key_of = jax.random.split(jax.random.key(seed), 9)
    grid_adjoint = scatter_about(key_of[0], (LAT, L, LON), 1.0, 6.0, ((0, 64), (1, 4)), jnp.float32)
    trajectory = scatter_about(key_of[1], (LAT, L, LON), 0.5, 3.0, ((0, 64), (1, 4)), jnp.float32)
    legendre_north = scatter_about(key_of[2], (M, M, LH), LH ** -0.5, 0.25, ((0, 256),), jnp.float32)
    slot_wavenumber = jax.random.permutation(key_of[3], M).astype(jnp.int32)
    spectral_state = scatter_about(key_of[4], (M, M, 2, L), 1.0, 6.0, ((0, 256),), jnp.float32)
    to_modes = scatter_about(key_of[5], (L, L), L ** -0.5, 0.75, (), jnp.float32)
    from_modes = scatter_about(key_of[6], (L, L), L ** -0.5, 0.75, (), jnp.float32)
    rates = jnp.clip(jnp.exp(jax.random.uniform(key_of[7], (L,), jnp.float32, math.log(0.1), math.log(10.0))), 0.1, 10.0)
    return dict(grid_adjoint=grid_adjoint, trajectory=trajectory, legendre_north=legendre_north, slot_wavenumber=slot_wavenumber, spectral_state=spectral_state, to_modes=to_modes, from_modes=from_modes, rates=rates)


def wave_table():
    column = jnp.arange(LON, dtype=jnp.int32)
    number = jnp.arange(M, dtype=jnp.int32)
    phase = (column[:, None] * number[None, :]) % LON
    angles = phase.astype(jnp.float32) * (2.0 * jnp.pi / LON)
    scale = jnp.float32(LON) ** -0.5
    return jnp.concatenate([jnp.cos(angles), -jnp.sin(angles)], axis=1) * scale


def unfold(north):
    depth = north.shape[0]
    parity = jnp.where(jnp.arange(depth) % 2 == 0, 1.0, -1.0).astype(jnp.float32)
    return jnp.concatenate([north, parity[:, None] * north[:, ::-1]], axis=1)


def reference(grid_adjoint, trajectory, legendre_north, slot_wavenumber, spectral_state, to_modes, from_modes, rates):
    highest = lax.Precision.HIGHEST
    table = wave_table()
    forced = grid_adjoint * (1.0 + trajectory)
    fourier = jnp.dot(forced.reshape(LAT * L, LON), table, precision=highest, preferred_element_type=jnp.float32)
    fourier = fourier.reshape(LAT, L, 2, M)
    slotted = jnp.take(fourier, slot_wavenumber, axis=3)
    columns = jnp.transpose(slotted, (3, 0, 1, 2))

    def analyse(pair):
        north, column_data = pair
        whole = unfold(north)
        return jnp.einsum('kt,tlc->kcl', whole, column_data, precision=highest)

    analysed = lax.map(analyse, (legendre_north, columns))
    depth_index = jnp.arange(M, dtype=jnp.int32)
    valid = (depth_index[None, :] < M - slot_wavenumber[:, None]).astype(jnp.float32)
    total = (analysed + spectral_state) * valid[:, :, None, None]
    degree = (slot_wavenumber[:, None] + depth_index[None, :]).astype(jnp.float32)
    helm = degree * (degree + 1.0) / (M * (M - 1.0))
    modes = jnp.einsum('skcl,pl->skcp', total, to_modes, precision=highest)
    scaled = modes / (1.0 + helm[:, :, None, None] * rates)
    spectral_out = jnp.einsum('skcp,lp->skcl', scaled, from_modes, precision=highest)

    def synthesise(pair):
        north, coeffs = pair
        whole = unfold(north)
        return jnp.einsum('kt,kcl->tlc', whole, coeffs, precision=highest)

    synthesised = lax.map(synthesise, (legendre_north, spectral_out))
    inverse = jnp.zeros((M,), jnp.int32).at[slot_wavenumber].set(jnp.arange(M, dtype=jnp.int32))
    ordered = jnp.transpose(jnp.take(synthesised, inverse, axis=0), (1, 2, 3, 0))
    grid_out = jnp.dot(ordered.reshape(LAT * L, 2 * M), table.T, precision=highest, preferred_element_type=jnp.float32)
    return spectral_out, grid_out.reshape(LAT, L, LON)
```

```python
import jax
import jax.numpy as jnp
import numpy as np
from jax import lax
from jax.experimental import pallas as pl
from jax.experimental.pallas import tpu as pltpu
from jax.sharding import PartitionSpec as P

WAVES = 512
LON = 2048
QUARTER = LON // 4
RESIDUES = (0, 2, 1, 3)
BF16 = jnp.bfloat16
F32 = jnp.float32


def wave_rows():
    j = np.arange(QUARTER, dtype=np.int64)
    blocks = []
    for residue in RESIDUES:
        m = 4 * np.arange(WAVES // 4, dtype=np.int64) + residue
        angle = (m[:, None] * j[None, :] % LON) * (2.0 * np.pi / LON)
        blocks += [np.cos(angle), -np.sin(angle)]
    table = (np.concatenate(blocks, axis=0) * LON**-0.5).astype(np.float32)
    high = table.astype(jnp.bfloat16)
    low = (table - high.astype(np.float32)).astype(jnp.bfloat16)
    return high, low


def split(value):
    high = value.astype(BF16)
    low = (value - high.astype(F32)).astype(BF16)
    return high, low


def mm(a, b):
    return lax.dot_general(a, b, (((1,), (0,)), ((), ())), preferred_element_type=F32)


def mm_nt(a, b):
    return lax.dot_general(a, b, (((1,), (1,)), ((), ())), preferred_element_type=F32)


def mm3(a, b):
    return mm(a[0], b[0]) + (mm(a[0], b[1]) + mm(a[1], b[0]))


def mm3_nt(a, b):
    return mm_nt(a[0], b[0]) + (mm_nt(a[0], b[1]) + mm_nt(a[1], b[0]))


def one_hot(slots_row):
    held = jnp.transpose(jnp.broadcast_to(slots_row.astype(F32), (128, WAVES)))
    lane = lax.broadcasted_iota(jnp.int32, (WAVES, 128), 1).astype(F32) * 4.0
    return jnp.concatenate(
        [(held == lane + float(r)).astype(F32).astype(BF16) for r in RESIDUES], axis=1
    )


def head_kernel(slots_ref, grid_ref, traj_ref, high_ref, low_ref, out_ref, work):
    half = QUARTER // 2
    for i in range(16):
        forced = grid_ref[i] * (1.0 + traj_ref[i])
        q0, q1, q2, q3 = (forced[:, QUARTER * q : QUARTER * (q + 1)] for q in range(4))
        even, swing = q0 + q2, q1 + q3
        rows = pl.ds(i, 16, stride=16)
        for n, part in enumerate((even + swing, even - swing, q0 - q2, q1 - q3)):
            for t in range(2 * half // 128):
                work[n, t, rows, :] = part[:, 128 * t : 128 * (t + 1)]
    full = lambda n: split(jnp.concatenate([work[n, t] for t in range(4)], axis=1))
    table = lambda a, b: (high_ref[a:b, :], low_ref[a:b, :])
    zero = mm3_nt(table(0, 256), full(0))
    two = mm3_nt(table(256, 512), full(1))
    odd = table(512, 1024)
    u1 = mm3_nt(odd, full(2))
    u2 = mm3_nt(odd, full(3))
    cosine = [zero[:128], two[:128], u1[:128] + u2[128:256], u1[256:384] - u2[384:]]
    sine = [zero[128:], two[128:], u1[128:256] - u2[:128], u1[384:] + u2[256:384]]
    pick = one_hot(slots_ref[...])
    for c, parts in enumerate((cosine, sine)):
        h, l = split(jnp.concatenate(parts, axis=0))
        slotted = mm(pick, h) + mm(pick, l)
        for k in range(2):
            out_ref[pl.ds(2 * k + c, WAVES, stride=4), :] = slotted[:, 128 * k : 128 * (k + 1)]


def prepare_kernel(slots_ref, p_ref, km_ref, kf_ref, ph_ref, pl_ref, th_ref, tl_ref, kh_ref, kl_ref, pick_ref):
    for s in range(2):
        value = p_ref[s]
        ph_ref[s], pl_ref[s] = split(value)
        th_ref[s], tl_ref[s] = split(jnp.transpose(value))
    kh_ref[0], kl_ref[0] = split(km_ref[...])
    kh_ref[1], kl_ref[1] = split(kf_ref[...])
    pick_ref[...] = one_hot(slots_ref[...])


def swap_groups(tiles, group):
    tiles = list(tiles)
    for bit in (1, 2, 4):
        mask = (group & bit) != 0
        for i in range(8):
            if i & bit:
                continue
            a, b = tiles[i], tiles[i | bit]
            tiles[i] = jnp.where(mask, pltpu.roll(b, 16 * bit, 1), a)
            tiles[i | bit] = jnp.where(mask, b, pltpu.roll(a, 128 - 16 * bit, 1))
    return tiles


def blocks_of(l_dim):
    return [(h * 64 + c * 32 + v * 8, c * 64 + v * 16 + h * 8) for c in range(2) for v in range(4) for h in range(2)]


def mid_kernel(
    waves_ref, y_ref, ph_ref, pl_ref, th_ref, tl_ref, kh_ref, kl_ref, scale_ref, state_ref,
    spectral_ref, z_ref, work,
):
    lane = lax.broadcasted_iota(jnp.int32, (8, 128), 1)
    group = lane // 16
    mirror = lane + 15 - 2 * (lane % 16)
    flip = lambda tile: jnp.take_along_axis(tile, mirror, axis=1)
    for v in range(4):
        for g in range(4):
            north = [y_ref[(8 * g + i) * 4 + v] for i in range(8)]
            south = [flip(y_ref[(63 - 8 * g - i) * 4 + v]) for i in range(8)]
            for par in range(2):
                folded = [n + s if par == 0 else n - s for n, s in zip(north, south)]
                for j, tile in enumerate(swap_groups(folded, group)):
                    work[par, g, pl.ds(v * 8 + j, 8, stride=32), :] = tile
    k_row = lax.broadcasted_iota(jnp.int32, (1, WAVES), 1)
    even_k = k_row % 2 == 0
    totals = []
    for s in range(2):
        rows = pl.ds(128 * s, 128)
        fold = [jnp.concatenate([work[par, g, rows, :] for g in range(4)], axis=1) for par in range(2)]
        both = mm3(split(jnp.concatenate(fold, axis=0)), (th_ref[s], tl_ref[s]))
        mixed = jnp.where(even_k, both[:128], both[128:])
        mixed = jnp.concatenate([mixed[a : a + 8] for a, _ in blocks_of(64)], axis=0)
        valid = (k_row < WAVES - waves_ref[s]).astype(F32)
        totals.append((mixed + state_ref[128 * s : 128 * (s + 1), :]) * valid)
    modes = mm3((kh_ref[0], kl_ref[0]), split(jnp.concatenate(totals, axis=0)))
    scales = [scale_ref[s] for s in (0, 0, 1, 1)]
    scaled = modes * jnp.concatenate(scales, axis=0)
    spectral = mm3((kh_ref[1], kl_ref[1]), split(scaled))
    spectral_ref[...] = spectral
    for s in range(2):
        own = spectral[128 * s : 128 * (s + 1)]
        pair = jnp.concatenate([jnp.where(even_k, own, 0.0), jnp.where(even_k, 0.0, own)], axis=0)
        both = mm3(split(pair), (ph_ref[s], pl_ref[s]))
        for par, side in enumerate((both[:128] + both[128:], both[:128] - both[128:])):
            for to, start in blocks_of(64):
                for g in range(4):
                    work[par, g, 128 * s + to : 128 * s + to + 8, :] = side[start : start + 8, 128 * g : 128 * (g + 1)]
    for v in range(4):
        for g in range(4):
            for par in range(2):
                tiles = [work[par, g, pl.ds(v * 8 + j, 8, stride=32), :] for j in range(8)]
                for i, tile in enumerate(swap_groups(tiles, group)):
                    if par == 0:
                        z_ref[(8 * g + i) * 4 + v] = tile
                    else:
                        z_ref[(63 - 8 * g - i) * 4 + v] = flip(tile)


def tail_kernel(z_ref, pick_ref, high_ref, low_ref, out_ref, work):
    pick = pick_ref[...]
    natural = []
    for c in range(2):
        sides = [z_ref[pl.ds(2 * k + c, WAVES, stride=4), :] for k in range(2)]
        h, l = split(jnp.transpose(jnp.concatenate(sides, axis=1)))
        natural.append(split(mm(h, pick) + mm(l, pick)))
    part = lambda c, kind: tuple(natural[c][n][:, 128 * kind : 128 * (kind + 1)] for n in range(2))
    minus = lambda pair: (-pair[0], -pair[1])
    join = lambda *parts: tuple(jnp.concatenate([p[n] for p in parts], axis=1) for n in range(2))
    table = lambda a, b: (high_ref[a:b, :], low_ref[a:b, :])
    zero = mm3(join(part(0, 0), part(1, 0)), table(0, 256))
    two = mm3(join(part(0, 1), part(1, 1)), table(256, 512))
    odd = table(512, 1024)
    first = mm3(join(part(0, 2), part(1, 2), part(0, 3), part(1, 3)), odd)
    turned = mm3(join(minus(part(1, 2)), part(0, 2), part(1, 3), minus(part(0, 3))), odd)
    plus, less = zero + two, zero - two
    for q, value in enumerate((plus + first, less + turned, plus - first, less - turned)):
        for t in range(4):
            work[4 * q + t] = value[:, 128 * t : 128 * (t + 1)]
    for t in range(16):
        for i in range(16):
            out_ref[i, :, 128 * t : 128 * (t + 1)] = work[t, pl.ds(i, 16, stride=16), :]


VMEM = pl.BlockSpec(memory_space=pltpu.VMEM)
SMEM = pl.BlockSpec(memory_space=pltpu.SMEM)


def call(kernel, name, outs, in_specs, scratch=(), flops=0, moved=0):
    return pl.pallas_call(
        kernel,
        name=name,
        out_shape=outs,
        in_specs=in_specs,
        out_specs=jax.tree.map(lambda _: VMEM, outs),
        scratch_shapes=list(scratch),
        compiler_params=pltpu.CompilerParams(vmem_limit_bytes=48 * 2**20),
        cost_estimate=pl.CostEstimate(flops=flops, bytes_accessed=moved, transcendentals=0),
    )


def shards(grid_adjoint, trajectory, legendre_north, slot_wavenumber, spectral_state, to_modes, from_modes, rates):
    shape = jax.ShapeDtypeStruct
    high, low = wave_rows()
    high, low = jnp.asarray(high), jnp.asarray(low)
    slots_row = slot_wavenumber.reshape(1, WAVES)
    device = lax.axis_index("band") * lax.axis_size("lev") + lax.axis_index("lev")
    own_waves = lax.dynamic_slice_in_dim(slot_wavenumber, 2 * device, 2)

    sent = call(
        head_kernel, "head", shape((2048, 128), F32), [VMEM] * 5,
        [pltpu.VMEM((4, 4, 256, 128), F32)], flops=2 * 10**9, moved=7 * 10**6,
    )(slots_row, grid_adjoint, trajectory, high, low)
    arrived = lax.all_to_all(sent.reshape(256, 8, 128), ("band", "lev"), 0, 0, tiled=True)

    k = jnp.arange(WAVES, dtype=jnp.int32)
    degree = (own_waves[:, None] + k[None, :]).astype(F32)
    helm = degree * (degree + 1.0) / (WAVES * (WAVES - 1.0))
    scale = 1.0 / (1.0 + helm[:, None, :] * rates[None, :, None])
    diagonal = jnp.eye(4, dtype=F32)
    outs = [shape((2, 512, 512), BF16)] * 4 + [shape((2, 256, 256), BF16)] * 2 + [shape((512, 512), BF16)]
    ph, plo, th, tl, kh, kl, pick = call(
        prepare_kernel, "prepare", outs, [VMEM] * 4, flops=10**8, moved=8 * 10**6
    )(slots_row, legendre_north, jnp.kron(diagonal, to_modes), jnp.kron(diagonal, from_modes))
    state = jnp.transpose(spectral_state, (0, 2, 3, 1)).reshape(256, WAVES)

    spectral, back = call(
        mid_kernel, "mid", [shape((256, WAVES), F32), shape((256, 8, 128), F32)], [SMEM] + [VMEM] * 9,
        [pltpu.VMEM((2, 4, 256, 128), F32)], flops=3 * 10**9, moved=8 * 10**6,
    )(own_waves, arrived, ph, plo, th, tl, kh, kl, scale, state)
    returned = lax.all_to_all(back, ("band", "lev"), 0, 0, tiled=True)
    grid = call(
        tail_kernel, "tail", shape((16, 16, LON), F32), [VMEM] * 4,
        [pltpu.VMEM((16, 256, 128), F32)], flops=2 * 10**9, moved=6 * 10**6,
    )(returned.reshape(2048, 128), pick, high, low)
    spectral_out = jnp.transpose(spectral.reshape(2, 2, 64, WAVES), (0, 3, 1, 2))
    return spectral_out, grid


def solution(mesh):
    spread = P(("band", "lev"), None, None)
    return jax.shard_map(
        shards,
        mesh=mesh,
        in_specs=(
            P("band", "lev", None), P("band", "lev", None), spread, P(),
            P(("band", "lev"), None, None, None), P(), P(), P(),
        ),
        out_specs=(P(("band", "lev"), None, None, None), P("band", "lev", None)),
        check_vma=False,
    )
```

```python
import jax
import jax.numpy as jnp
import numpy as np
from jax import lax
from jax.experimental import pallas as pl
from jax.experimental.pallas import tpu as pltpu
from jax.sharding import PartitionSpec as P

WAVES = 512
LON = 2048
QUARTER = LON // 4
RESIDUES = (0, 2, 1, 3)
BF16 = jnp.bfloat16
F32 = jnp.float32


def wave_rows():
    j = np.arange(QUARTER, dtype=np.int64)
    blocks = []
    for residue in RESIDUES:
        m = 4 * np.arange(WAVES // 4, dtype=np.int64) + residue
        angle = (m[:, None] * j[None, :] % LON) * (2.0 * np.pi / LON)
        blocks += [np.cos(angle), -np.sin(angle)]
    table = (np.concatenate(blocks, axis=0) * LON**-0.5).astype(np.float32)
    high = table.astype(jnp.bfloat16)
    low = (table - high.astype(np.float32)).astype(jnp.bfloat16)
    return high, low


def split(value):
    high = value.astype(BF16)
    low = (value - high.astype(F32)).astype(BF16)
    return high, low


def mm(a, b):
    return lax.dot_general(a, b, (((1,), (0,)), ((), ())), preferred_element_type=F32)


def mm_nt(a, b):
    return lax.dot_general(a, b, (((1,), (1,)), ((), ())), preferred_element_type=F32)


def mm3(a, b):
    return mm(a[0], b[0]) + (mm(a[0], b[1]) + mm(a[1], b[0]))


def mm3_nt(a, b):
    return mm_nt(a[0], b[0]) + (mm_nt(a[0], b[1]) + mm_nt(a[1], b[0]))


def one_hot(slots_row):
    held = jnp.transpose(jnp.broadcast_to(slots_row.astype(F32), (128, WAVES)))
    lane = lax.broadcasted_iota(jnp.int32, (WAVES, 128), 1).astype(F32) * 4.0
    return jnp.concatenate(
        [(held == lane + float(r)).astype(F32).astype(BF16) for r in RESIDUES], axis=1
    )


def head_kernel(
    slots_ref, grid_hbm, traj_hbm, high_hbm, low_hbm, out_hbm,
    grid_ref, traj_ref, high_ref, low_ref, parts, sent, sems,
):
    copies = []
    for t in range(16):
        columns = pl.ds(128 * (4 * (t % 4) + t // 4), 128)
        for k, (src, dst) in enumerate(((grid_hbm, grid_ref), (traj_hbm, traj_ref))):
            copies.append(pltpu.make_async_copy(src.at[:, columns], dst.at[t], sems.at[2 * t + k]))
    tables = [
        pltpu.make_async_copy(src, dst, sems.at[32 + k])
        for k, (src, dst) in enumerate(((high_hbm, high_ref), (low_hbm, low_ref)))
    ]
    for copy in copies + tables:
        copy.start()
    pick = one_hot(slots_ref[...])
    for t in range(4):
        for copy in copies[8 * t : 8 * t + 8]:
            copy.wait()
        lanes = pl.ds(128 * t, 128)
        for level in range(16):
            lats = pl.ds(level, 16, stride=16)
            q0, q1, q2, q3 = (
                grid_ref[4 * t + q, lats, :] * (1.0 + traj_ref[4 * t + q, lats, :]) for q in range(4)
            )
            even, swing = q0 + q2, q1 + q3
            rows = pl.ds(16 * level, 16)
            for n, part in enumerate((even + swing, even - swing, q0 - q2, q1 - q3)):
                parts[n, 0, rows, lanes], parts[n, 1, rows, lanes] = split(part)
    for copy in tables:
        copy.wait()

    def product(a, b, n):
        count = b - a
        both = jnp.concatenate([high_ref[a:b, :], low_ref[a:b, :]], axis=0)
        wide = mm_nt(both, parts[n, 0])
        return wide[:count] + wide[count:] + mm_nt(high_ref[a:b, :], parts[n, 1])

    zero, two, u1, u2 = product(0, 256, 0), product(256, 512, 1), product(512, 1024, 2), product(512, 1024, 3)
    cosine = [zero[:128], two[:128], u1[:128] + u2[128:256], u1[256:384] - u2[384:]]
    sine = [zero[128:], two[128:], u1[128:256] - u2[:128], u1[384:] + u2[256:384]]
    sides = [split(jnp.concatenate(wave, axis=0)) for wave in (cosine, sine)]
    wide = jnp.concatenate([sides[0][0], sides[1][0], sides[0][1], sides[1][1]], axis=1)
    stores = []
    for n in range(4):
        found = mm(pick[128 * n : 128 * (n + 1)], wide)
        found = found[:, :512] + found[:, 512:]
        for c in range(2):
            for k in range(2):
                sent[pl.ds(512 * n + 2 * k + c, 128, stride=4), :] = found[:, 256 * c + 128 * k : 256 * c + 128 * (k + 1)]
        rows = pl.ds(512 * n, 512)
        stores.append(pltpu.make_async_copy(sent.at[rows], out_hbm.at[rows], sems.at[34 + n]))
        stores[-1].start()
    for copy in stores:
        copy.wait()


def prepare_kernel(slots_ref, p_ref, high_ref, low_ref, pick_ref):
    for s in range(2):
        high_ref[s], low_ref[s] = split(p_ref[s])
    pick_ref[...] = one_hot(slots_ref[...])


def swap_groups(tiles, group):
    tiles = list(tiles)
    for bit in (1, 2, 4):
        mask = (group & bit) != 0
        for i in range(8):
            if i & bit:
                continue
            a, b = tiles[i], tiles[i | bit]
            tiles[i] = jnp.where(mask, pltpu.roll(b, 16 * bit, 1), a)
            tiles[i | bit] = jnp.where(mask, b, pltpu.roll(a, 128 - 16 * bit, 1))
    return tiles


def mid_kernel(
    waves_ref, rates_ref, to_ref, from_ref, y_ref, ph_hbm, pl_hbm, state_hbm,
    spectral_hbm, z_ref,
    ph_ref, pl_ref, state_ref, spectral_ref, folds, north, south, sems,
):
    sources, targets = (ph_hbm, pl_hbm, state_hbm), (ph_ref, pl_ref, state_ref)
    copies = [pltpu.make_async_copy(a, b, sems.at[k]) for k, (a, b) in enumerate(zip(sources, targets))]
    for copy in copies:
        copy.start()
    lane = lax.broadcasted_iota(jnp.int32, (8, 128), 1)
    group = lane // 16
    mirror = lane + 15 - 2 * (lane % 16)
    flip = lambda tile: jnp.take_along_axis(tile, mirror, axis=1)

    def fold_step(step, carry):
        v, g = step // 4, step % 4
        ahead = swap_groups([y_ref[(8 * g + i) * 4 + v] for i in range(8)], group)
        behind = swap_groups([y_ref[(63 - 8 * g - i) * 4 + v] for i in range(8)], group)
        for j in range(8):
            a, b = ahead[j], flip(behind[j])
            rows = pl.ds(pl.multiple_of(64 * v + 8 * j, 8), 8)
            folds[0, g, rows, :] = a + b
            folds[1, g, rows, :] = a - b
        return carry

    lax.fori_loop(0, 16, fold_step, 0, unroll=4)
    k_row = lax.broadcasted_iota(jnp.int32, (1, WAVES), 1)
    even_k = k_row % 2 == 0
    to_modes, from_modes = split(to_ref[...]), split(from_ref[...])
    rate = jnp.broadcast_to(rates_ref[:, 0:1], (64, WAVES))
    for copy in copies:
        copy.wait()
    pick_rows = lambda pair, rows: tuple(p[rows] for p in pair)
    for s in range(2):
        fold = []
        for par in range(2):
            for c in range(2):
                halves = [
                    jnp.concatenate(
                        [folds[par, g, pl.ds(4 * s + 2 * h + c, 32, stride=8), :] for g in range(4)], axis=1
                    )
                    for h in range(2)
                ]
                fold += [halves[h][8 * v : 8 * v + 8] for v in range(4) for h in range(2)]
        both = mm3_nt(split(jnp.concatenate(fold, axis=0)), (ph_ref[s], pl_ref[s]))
        wave = waves_ref[s]
        valid = (k_row < WAVES - wave).astype(F32)
        degree = (k_row + wave).astype(F32)
        helm = degree * (degree + 1.0) / (WAVES * (WAVES - 1.0))
        scale = 1.0 / (1.0 + helm * rate)
        for c in range(2):
            rows = pl.ds(128 * s + 64 * c, 64)
            mixed = jnp.where(even_k, both[64 * c : 64 * c + 64], both[128 + 64 * c : 192 + 64 * c])
            total = (mixed + state_ref[rows, :]) * valid
            modes = mm3(to_modes, split(total)) * scale
            spectral_ref[rows, :] = mm3(from_modes, split(modes))
    store = pltpu.make_async_copy(spectral_ref, spectral_hbm, sems.at[3])
    store.start()
    for s in range(2):
        own = spectral_ref[128 * s : 128 * (s + 1), :]
        pair = jnp.concatenate([jnp.where(even_k, own, 0.0), jnp.where(even_k, 0.0, own)], axis=0)
        both = mm3(split(pair), (ph_ref[s], pl_ref[s]))
        for to, side in ((north, both[:128] + both[128:]), (south, both[:128] - both[128:])):
            for c in range(2):
                for v in range(4):
                    for h in range(2):
                        row, start = 128 * s + 64 * h + 32 * c + 8 * v, 64 * c + 16 * v + 8 * h
                        for g in range(4):
                            to[g, row : row + 8, :] = side[start : start + 8, 128 * g : 128 * (g + 1)]
    for v in range(4):
        for g in range(4):
            for side in (north, south):
                tiles = [side[g, pl.ds(v * 8 + j, 8, stride=32), :] for j in range(8)]
                for i, tile in enumerate(swap_groups(tiles, group)):
                    if side is north:
                        z_ref[(8 * g + i) * 4 + v] = tile
                    else:
                        z_ref[(63 - 8 * g - i) * 4 + v] = flip(tile)
    store.wait()


def tail_kernel(z_ref, pick_ref, high_ref, low_ref, out_hbm, work, block, sems):
    pick = pick_ref[...]
    natural = []
    for c in range(2):
        sides = [z_ref[pl.ds(2 * k + c, WAVES, stride=4), :] for k in range(2)]
        h, l = split(jnp.transpose(jnp.concatenate(sides, axis=1)))
        natural.append(split(mm(h, pick) + mm(l, pick)))
    part = lambda c, kind: tuple(natural[c][n][:, 128 * kind : 128 * (kind + 1)] for n in range(2))
    minus = lambda pair: (-pair[0], -pair[1])
    join = lambda *parts: tuple(jnp.concatenate([p[n] for p in parts], axis=1) for n in range(2))
    table = lambda a, b: (high_ref[a:b, :], low_ref[a:b, :])
    zero = mm3(join(part(0, 0), part(1, 0)), table(0, 256))
    two = mm3(join(part(0, 1), part(1, 1)), table(256, 512))
    odd = table(512, 1024)
    stores = []

    def put(q, value):
        for t in range(4):
            work[4 * q + t] = value[:, 128 * t : 128 * (t + 1)]
        for i in range(16):
            for t in range(4 * q, 4 * q + 4):
                block[i, :, 128 * t : 128 * (t + 1)] = work[t, pl.ds(i, 16, stride=16), :]
        columns = pl.ds(QUARTER * q, QUARTER)
        stores.append(pltpu.make_async_copy(block.at[:, :, columns], out_hbm.at[:, :, columns], sems.at[q]))
        stores[-1].start()

    plus, less = zero + two, zero - two
    first = mm3(join(part(0, 2), part(1, 2), part(0, 3), part(1, 3)), odd)
    put(0, plus + first)
    put(2, plus - first)
    turned = mm3(join(minus(part(1, 2)), part(0, 2), part(1, 3), minus(part(0, 3))), odd)
    put(1, less + turned)
    put(3, less - turned)
    for copy in stores:
        copy.wait()


VMEM = pl.BlockSpec(memory_space=pltpu.VMEM)
SMEM = pl.BlockSpec(memory_space=pltpu.SMEM)
HBM = pl.BlockSpec(memory_space=pltpu.HBM)
DMA = pltpu.SemaphoreType.DMA


def call(kernel, name, outs, in_specs, out_specs, scratch=(), flops=0, moved=0, room=32):
    return pl.pallas_call(
        kernel,
        name=name,
        out_shape=outs,
        in_specs=in_specs,
        out_specs=out_specs,
        scratch_shapes=list(scratch),
        compiler_params=pltpu.CompilerParams(vmem_limit_bytes=room * 2**20),
        cost_estimate=pl.CostEstimate(flops=flops, bytes_accessed=moved, transcendentals=0),
    )


def shards(grid_adjoint, trajectory, legendre_north, slot_wavenumber, spectral_state, to_modes, from_modes, rates):
    shape = jax.ShapeDtypeStruct
    high, low = wave_rows()
    high, low = jnp.asarray(high), jnp.asarray(low)
    slots_row = slot_wavenumber.reshape(1, WAVES)
    device = lax.axis_index("band") * lax.axis_size("lev") + lax.axis_index("lev")
    own_waves = lax.dynamic_slice_in_dim(slot_wavenumber, 2 * device, 2)

    square = (256, LON)
    sent = call(
        head_kernel, "head", shape((2048, 128), F32), [VMEM] + [HBM] * 4, HBM,
        [pltpu.VMEM((16, 256, 128), F32)] * 2 + [pltpu.VMEM((1024, QUARTER), BF16)] * 2
        + [pltpu.VMEM((4, 2, 256, QUARTER), BF16), pltpu.VMEM((2048, 128), F32), DMA((38,))],
        flops=2 * 10**9, moved=7 * 10**6, room=60,
    )(slots_row, grid_adjoint.reshape(square), trajectory.reshape(square), high, low)
    arrived = lax.all_to_all(sent.reshape(256, 8, 128), ("band", "lev"), 0, 0, tiled=True)

    ph, plo, pick = call(
        prepare_kernel, "prepare", [shape((2, 512, 512), BF16)] * 2 + [shape((512, 512), BF16)],
        [VMEM] * 2, [VMEM] * 3, flops=10**8, moved=8 * 10**6,
    )(slots_row, legendre_north)
    state = jnp.transpose(spectral_state, (0, 2, 3, 1)).reshape(256, WAVES)
    columns = jnp.broadcast_to(rates[:, None], (64, 128))
    far = [pltpu.with_memory_space_constraint(v, pltpu.HBM) for v in (ph, plo, state)]

    legendre, rows = pltpu.VMEM((2, 512, 512), BF16), pltpu.VMEM((256, WAVES), F32)
    spectral, back = call(
        mid_kernel, "mid", [shape((256, WAVES), F32), shape((256, 8, 128), F32)],
        [SMEM] + [VMEM] * 4 + [HBM] * 3, [HBM, VMEM],
        [legendre, legendre, rows, rows, pltpu.VMEM((2, 4, 256, 128), F32)]
        + [pltpu.VMEM((4, 256, 128), F32)] * 2 + [DMA((4,))],
        flops=3 * 10**9, moved=8 * 10**6, room=32,
    )(own_waves, columns, to_modes, from_modes, arrived, *far)
    returned = lax.all_to_all(back, ("band", "lev"), 0, 0, tiled=True)
    grid = call(
        tail_kernel, "tail", shape((16, 16, LON), F32), [VMEM] * 4, HBM,
        [pltpu.VMEM((16, 256, 128), F32), pltpu.VMEM((16, 16, LON), F32), DMA((4,))],
        flops=2 * 10**9, moved=6 * 10**6,
    )(returned.reshape(2048, 128), pick, high, low)
    spectral_out = jnp.transpose(spectral.reshape(2, 2, 64, WAVES), (0, 3, 1, 2))
    return spectral_out, grid


def solution(mesh):
    spread = P(("band", "lev"), None, None)
    return jax.shard_map(
        shards,
        mesh=mesh,
        in_specs=(
            P("band", "lev", None), P("band", "lev", None), spread, P(),
            P(("band", "lev"), None, None, None), P(), P(), P(),
        ),
        out_specs=(P(("band", "lev"), None, None, None), P("band", "lev", None)),
        check_vma=False,
    )
```

```python
import jax
import jax.numpy as jnp
import numpy as np
from jax import lax
from jax.experimental import pallas as pl
from jax.experimental.pallas import tpu as pltpu
from jax.sharding import PartitionSpec as P

WAVES = 512
LON = 2048
QUARTER = LON // 4
RESIDUES = (0, 2, 1, 3)
BF16 = jnp.bfloat16
F32 = jnp.float32


def wave_rows():
    j = np.arange(QUARTER, dtype=np.int64)
    blocks = []
    for residue in RESIDUES:
        m = 4 * np.arange(WAVES // 4, dtype=np.int64) + residue
        angle = (m[:, None] * j[None, :] % LON) * (2.0 * np.pi / LON)
        blocks += [np.cos(angle), -np.sin(angle)]
    table = (np.concatenate(blocks, axis=0) * LON**-0.5).astype(np.float32)
    table = np.stack([table[:, : QUARTER // 2], table[:, QUARTER // 2 :]])
    high = table.astype(jnp.bfloat16)
    low = (table - high.astype(np.float32)).astype(jnp.bfloat16)
    return high, low


def split(value):
    high = value.astype(BF16)
    low = (value - high.astype(F32)).astype(BF16)
    return high, low


def mm(a, b):
    return lax.dot_general(a, b, (((1,), (0,)), ((), ())), preferred_element_type=F32)


def mm_nt(a, b):
    return lax.dot_general(a, b, (((1,), (1,)), ((), ())), preferred_element_type=F32)


def mm3(a, b):
    return mm(a[0], b[0]) + (mm(a[0], b[1]) + mm(a[1], b[0]))


def mm3_nt(a, b):
    return mm_nt(a[0], b[0]) + (mm_nt(a[0], b[1]) + mm_nt(a[1], b[0]))


def one_hot(slots_row):
    held = jnp.transpose(jnp.broadcast_to(slots_row.astype(F32), (128, WAVES)))
    lane = lax.broadcasted_iota(jnp.int32, (WAVES, 128), 1).astype(F32) * 4.0
    return jnp.concatenate(
        [(held == lane + float(r)).astype(F32).astype(BF16) for r in RESIDUES], axis=1
    )


def head_kernel(
    slots_hbm, grid_hbm, traj_hbm, high_hbm, low_hbm, out_hbm,
    slots_ref, grid_ref, traj_ref, high_ref, low_ref, parts, sent, sems,
):
    slots = pltpu.make_async_copy(slots_hbm, slots_ref, sems.at[40])
    slots.start()
    inputs, tables = [], []
    for half in range(2):
        for q in range(4):
            columns, at = pl.ds(QUARTER * q + QUARTER // 2 * half, QUARTER // 2), 4 * half + q
            for k, (src, dst) in enumerate(((grid_hbm, grid_ref), (traj_hbm, traj_ref))):
                inputs.append(pltpu.make_async_copy(src.at[:, columns], dst.at[at], sems.at[2 * at + k]))
                inputs[-1].start()
        for k, (src, dst) in enumerate(((high_hbm, high_ref), (low_hbm, low_ref))):
            tables.append(pltpu.make_async_copy(src.at[half], dst.at[half], sems.at[32 + 2 * half + k]))
            tables[-1].start()
    slots.wait()
    pick = one_hot(slots_ref[...])

    def product(half, a, b, n):
        count = b - a
        both = jnp.concatenate([high_ref[half, a:b, :], low_ref[half, a:b, :]], axis=0)
        wide = mm_nt(both, parts[half, n, 0])
        return wide[:count] + wide[count:] + mm_nt(high_ref[half, a:b, :], parts[half, n, 1])

    def fetch(half):
        for copy in inputs[8 * half : 8 * half + 8] + tables[2 * half : 2 * half + 2]:
            copy.wait()

    def combine(half):
        for lat in range(0, 16, 2):
            for h in range(2):
                quarters = []
                for q in range(4):
                    picked = [
                        jnp.concatenate([ref[4 * half + q, 16 * n + 8 * h : 16 * n + 8 * h + 8, :] for n in (lat, lat + 1)])
                        for ref in (grid_ref, traj_ref)
                    ]
                    quarters.append(picked[0] * (1.0 + picked[1]))
                q0, q1, q2, q3 = quarters
                even, swing = q0 + q2, q1 + q3
                rows = pl.ds(128 * h + 8 * lat, 16)
                for n, part in enumerate((even + swing, even - swing, q0 - q2, q1 - q3)):
                    parts[half, n, 0, rows, :], parts[half, n, 1, rows, :] = split(part)

    def products(half):
        return [product(half, a, b, n) for n, (a, b) in enumerate(((0, 256), (256, 512), (512, 1024), (512, 1024)))]

    fetch(0)
    combine(0)
    sums = products(0)
    fetch(1)
    combine(1)
    sums = [x + y for x, y in zip(sums, products(1))]
    zero, two, u1, u2 = sums
    cosine = [zero[:128], two[:128], u1[:128] + u2[128:256], u1[256:384] - u2[384:]]
    sine = [zero[128:], two[128:], u1[128:256] - u2[:128], u1[384:] + u2[256:384]]
    sides = [split(jnp.concatenate(wave, axis=0)) for wave in (cosine, sine)]
    wide = jnp.concatenate([sides[0][0], sides[1][0], sides[0][1], sides[1][1]], axis=1)
    stores = []
    for n in range(4):
        found = mm(pick[128 * n : 128 * (n + 1)], wide)
        found = found[:, :512] + found[:, 512:]
        for c in range(2):
            for k in range(2):
                sent[pl.ds(512 * n + 2 * k + c, 128, stride=4), :] = found[:, 256 * c + 128 * k : 256 * c + 128 * (k + 1)]
        rows = pl.ds(512 * n, 512)
        stores.append(pltpu.make_async_copy(sent.at[rows], out_hbm.at[rows], sems.at[36 + n]))
        stores[-1].start()
    for copy in stores:
        copy.wait()


def prepare_kernel(slots_ref, p_ref, to_ref, from_ref, high_ref, low_ref, pick_ref, couple_ref):
    for n, ref in enumerate((to_ref, from_ref)):
        high, low = split(ref[...])
        couple_ref[n] = jnp.concatenate([high, high, low], axis=1)
    source = lax.broadcasted_iota(jnp.int32, (128, 128), 0)
    target = lax.broadcasted_iota(jnp.int32, (128, 128), 1)
    order = (source == (target % 8) * 16 + target // 8).astype(F32).astype(BF16)
    for s in range(2):
        for ref, value in zip((high_ref, low_ref), split(p_ref[s])):
            for g in range(4):
                lanes = slice(128 * g, 128 * (g + 1))
                ref[s, :, lanes] = mm(value[:, lanes], order).astype(BF16)
    pick_ref[...] = one_hot(slots_ref[...])


def swap_groups(tiles, lane):
    tiles = list(tiles)
    for bit in (1, 2, 4):
        mask = (lane & bit) != 0
        for i in range(8):
            if i & bit:
                continue
            a, b = tiles[i], tiles[i | bit]
            moved = jnp.take_along_axis(jnp.where(mask, a, b), lane ^ bit, axis=1)
            tiles[i], tiles[i | bit] = jnp.where(mask, moved, a), jnp.where(mask, b, moved)
    return tiles


def mid_kernel(
    waves_ref, rates_ref, couple_ref, y_ref, ph_hbm, pl_hbm, state_hbm,
    spectral_hbm, z_ref,
    ph_ref, pl_ref, state_ref, spectral_ref, scale_ref, folds, north, south, sems,
):
    sources, targets = (ph_hbm, pl_hbm, state_hbm), (ph_ref, pl_ref, state_ref)
    copies = [pltpu.make_async_copy(a, b, sems.at[k]) for k, (a, b) in enumerate(zip(sources, targets))]
    for copy in copies:
        copy.start()
    lane = lax.broadcasted_iota(jnp.int32, (8, 128), 1)
    mirror = lane ^ 120
    flip = lambda tile: jnp.take_along_axis(tile, mirror, axis=1)

    def fold_step(step, carry):
        v, g = step // 4, step % 4
        ahead = swap_groups([y_ref[(8 * g + i) * 4 + v] for i in range(8)], lane)
        behind = swap_groups([y_ref[(63 - 8 * g - i) * 4 + v] for i in range(8)], lane)
        for j in range(8):
            a, b = ahead[j], flip(behind[j])
            rows = pl.ds(pl.multiple_of(64 * v + 8 * j, 8), 8)
            folds[0, g, rows, :] = a + b
            folds[1, g, rows, :] = a - b
        return carry

    lax.fori_loop(0, 16, fold_step, 0, unroll=4)
    k_row = lax.broadcasted_iota(jnp.int32, (1, WAVES), 1)
    even_k = k_row % 2 == 0
    rate = jnp.broadcast_to(rates_ref[:, 0:1], (64, WAVES))
    for s in range(2):
        degree = (k_row + waves_ref[s : s + 1, :]).astype(F32)
        helm = degree * (degree + 1.0) / (WAVES * (WAVES - 1.0))
        scale_ref[s] = 1.0 / (1.0 + helm * rate)
    for copy in copies:
        copy.wait()
    totals = []
    for s in range(2):
        fold = []
        for par in range(2):
            for c in range(2):
                halves = [
                    jnp.concatenate(
                        [folds[par, g, pl.ds(4 * s + 2 * h + c, 32, stride=8), :] for g in range(4)], axis=1
                    )
                    for h in range(2)
                ]
                fold += [halves[h][8 * v : 8 * v + 8] for v in range(4) for h in range(2)]
        both = mm3_nt(split(jnp.concatenate(fold, axis=0)), (ph_ref[s], pl_ref[s]))
        valid = (k_row < WAVES - waves_ref[s : s + 1, :]).astype(F32)
        mixed = jnp.where(even_k, both[:128], both[128:])
        total = (mixed + state_ref[pl.ds(128 * s, 128), :]) * valid
        totals += [total[:64], total[64:]]
    h, l = split(jnp.concatenate(totals, axis=1))
    modes = mm(couple_ref[0], jnp.concatenate([h, l, h], axis=0))
    scales = [scale_ref[s] for s in (0, 0, 1, 1)]
    h, l = split(modes * jnp.concatenate(scales, axis=1))
    spectral = mm(couple_ref[1], jnp.concatenate([h, l, h], axis=0))
    for n in range(4):
        spectral_ref[pl.ds(64 * n, 64), :] = spectral[:, WAVES * n : WAVES * (n + 1)]
    store = pltpu.make_async_copy(spectral_ref, spectral_hbm, sems.at[3])
    store.start()
    for s in range(2):
        own = spectral_ref[128 * s : 128 * (s + 1), :]
        pair = jnp.concatenate([jnp.where(even_k, own, 0.0), jnp.where(even_k, 0.0, own)], axis=0)
        both = mm3(split(pair), (ph_ref[s], pl_ref[s]))
        for to, side in ((north, both[:128] + both[128:]), (south, both[:128] - both[128:])):
            for c in range(2):
                for v in range(4):
                    for h in range(2):
                        row, start = 128 * s + 64 * h + 32 * c + 8 * v, 64 * c + 16 * v + 8 * h
                        for g in range(4):
                            to[g, row : row + 8, :] = side[start : start + 8, 128 * g : 128 * (g + 1)]
    for v in range(4):
        for g in range(4):
            for side in (north, south):
                tiles = [side[g, pl.ds(v * 8 + j, 8, stride=32), :] for j in range(8)]
                for i, tile in enumerate(swap_groups(tiles, lane)):
                    if side is north:
                        z_ref[(8 * g + i) * 4 + v] = tile
                    else:
                        z_ref[(63 - 8 * g - i) * 4 + v] = flip(tile)
    store.wait()


def tail_kernel(z_ref, pick_ref, high_ref, low_ref, out_hbm, block, sems):
    pick = pick_ref[...]
    natural = []
    for c in range(2):
        sides = [z_ref[pl.ds(2 * k + c, WAVES, stride=4), :] for k in range(2)]
        h, l = split(jnp.transpose(jnp.concatenate(sides, axis=1)))
        natural.append(split(mm(h, pick) + mm(l, pick)))
    part = lambda c, kind: tuple(natural[c][n][:, 128 * kind : 128 * (kind + 1)] for n in range(2))
    minus = lambda pair: (-pair[0], -pair[1])
    join = lambda *parts: tuple(jnp.concatenate([p[n] for p in parts], axis=1) for n in range(2))
    whole = lambda ref, a, b: jnp.concatenate([ref[0, a:b, :], ref[1, a:b, :]], axis=1)
    table = lambda a, b: (whole(high_ref, a, b), whole(low_ref, a, b))
    zero = mm3(join(part(0, 0), part(1, 0)), table(0, 256))
    two = mm3(join(part(0, 1), part(1, 1)), table(256, 512))
    odd = table(512, 1024)
    stores = []

    def put(q, value):
        for h in range(2):
            for lat in range(16):
                row = 128 * h + 8 * lat
                block[lat, 8 * h : 8 * h + 8, QUARTER * q : QUARTER * (q + 1)] = value[row : row + 8]
        columns = pl.ds(QUARTER * q, QUARTER)
        stores.append(pltpu.make_async_copy(block.at[:, :, columns], out_hbm.at[:, :, columns], sems.at[q]))
        stores[-1].start()

    plus, less = zero + two, zero - two
    first = mm3(join(part(0, 2), part(1, 2), part(0, 3), part(1, 3)), odd)
    put(0, plus + first)
    put(2, plus - first)
    turned = mm3(join(minus(part(1, 2)), part(0, 2), part(1, 3), minus(part(0, 3))), odd)
    put(1, less + turned)
    put(3, less - turned)
    for copy in stores:
        copy.wait()


VMEM = pl.BlockSpec(memory_space=pltpu.VMEM)
HBM = pl.BlockSpec(memory_space=pltpu.HBM)
DMA = pltpu.SemaphoreType.DMA


def call(kernel, name, outs, in_specs, out_specs, scratch=(), flops=0, moved=0, room=32):
    return pl.pallas_call(
        kernel,
        name=name,
        out_shape=outs,
        in_specs=in_specs,
        out_specs=out_specs,
        scratch_shapes=list(scratch),
        compiler_params=pltpu.CompilerParams(vmem_limit_bytes=room * 2**20),
        cost_estimate=pl.CostEstimate(flops=flops, bytes_accessed=moved, transcendentals=0),
    )


def shards(grid_adjoint, trajectory, legendre_north, slot_wavenumber, spectral_state, to_modes, from_modes, rates):
    shape = jax.ShapeDtypeStruct
    high, low = wave_rows()
    high, low = jnp.asarray(high), jnp.asarray(low)
    slots_row = slot_wavenumber.reshape(1, WAVES)
    device = lax.axis_index("band") * lax.axis_size("lev") + lax.axis_index("lev")
    own_waves = lax.dynamic_slice_in_dim(slot_wavenumber, 2 * device, 2)

    square = (256, LON)
    sent = call(
        head_kernel, "head", shape((2048, 128), F32), [HBM] * 5, HBM,
        [pltpu.VMEM((1, WAVES), jnp.int32)] + [pltpu.VMEM((8, 256, QUARTER // 2), F32)] * 2 + [pltpu.VMEM((2, 1024, QUARTER // 2), BF16)] * 2
        + [pltpu.VMEM((2, 4, 2, 256, QUARTER // 2), BF16), pltpu.VMEM((2048, 128), F32), DMA((41,))],
        flops=2 * 10**9, moved=7 * 10**6, room=60,
    )(slots_row, grid_adjoint.reshape(square), trajectory.reshape(square), high, low)
    arrived = lax.all_to_all(sent.reshape(256, 8, 128), ("band", "lev"), 0, 0, tiled=True)

    ph, plo, pick, couple = call(
        prepare_kernel, "prepare",
        [shape((2, 512, 512), BF16)] * 2 + [shape((512, 512), BF16), shape((2, 64, 192), BF16)],
        [VMEM] * 4, [VMEM] * 4, flops=10**8, moved=8 * 10**6,
    )(slots_row, legendre_north, to_modes, from_modes)
    state = jnp.transpose(spectral_state, (0, 2, 3, 1)).reshape(256, WAVES)
    columns = jnp.broadcast_to(rates[:, None], (64, 128))
    far = [pltpu.with_memory_space_constraint(v, pltpu.HBM) for v in (ph, plo, state)]

    legendre, rows = pltpu.VMEM((2, 512, 512), BF16), pltpu.VMEM((256, WAVES), F32)
    spectral, back = call(
        mid_kernel, "mid", [shape((256, WAVES), F32), shape((256, 8, 128), F32)],
        [VMEM] * 4 + [HBM] * 3, [HBM, VMEM],
        [legendre, legendre, rows, rows, pltpu.VMEM((2, 64, WAVES), F32), pltpu.VMEM((2, 4, 256, 128), F32)]
        + [pltpu.VMEM((4, 256, 128), F32)] * 2 + [DMA((4,))],
        flops=3 * 10**9, moved=8 * 10**6, room=32,
    )(jnp.broadcast_to(own_waves[:, None], (2, WAVES)), columns, couple, arrived, *far)
    returned = lax.all_to_all(back, ("band", "lev"), 0, 0, tiled=True)
    grid = call(
        tail_kernel, "tail", shape((16, 16, LON), F32), [VMEM] * 4, HBM,
        [pltpu.VMEM((16, 16, LON), F32), DMA((4,))],
        flops=2 * 10**9, moved=6 * 10**6,
    )(returned.reshape(2048, 128), pick, high, low)
    spectral_out = jnp.transpose(spectral.reshape(2, 2, 64, WAVES), (0, 3, 1, 2))
    return spectral_out, grid


def solution(mesh):
    spread = P(("band", "lev"), None, None)
    return jax.shard_map(
        shards,
        mesh=mesh,
        in_specs=(
            P("band", "lev", None), P("band", "lev", None), spread, P(),
            P(("band", "lev"), None, None, None), P(), P(), P(),
        ),
        out_specs=(P(("band", "lev"), None, None, None), P("band", "lev", None)),
        check_vma=False,
    )
```

```python
import jax
import jax.numpy as jnp
import numpy as np
from jax import lax
from jax.experimental import pallas as pl
from jax.experimental.pallas import tpu as pltpu
from jax.sharding import PartitionSpec as P

WAVES = 512
LON = 2048
QUARTER = LON // 4
RESIDUES = (0, 2, 1, 3)
PITCH = 40
BF16 = jnp.bfloat16
F32 = jnp.float32


def wave_rows():
    j = np.arange(QUARTER, dtype=np.int64)
    blocks = []
    for residue in RESIDUES:
        m = 4 * np.arange(WAVES // 4, dtype=np.int64) + residue
        angle = (m[:, None] * j[None, :] % LON) * (2.0 * np.pi / LON)
        blocks += [np.cos(angle), -np.sin(angle)]
    table = (np.concatenate(blocks, axis=0) * LON**-0.5).astype(np.float32)
    table = np.stack([table[:, : QUARTER // 2], table[:, QUARTER // 2 :]])
    high = table.astype(jnp.bfloat16)
    low = (table - high.astype(np.float32)).astype(jnp.bfloat16)
    return high, low


def split(value):
    high = value.astype(BF16)
    low = (value - high.astype(F32)).astype(BF16)
    return high, low


def mm(a, b):
    return lax.dot_general(a, b, (((1,), (0,)), ((), ())), preferred_element_type=F32)


def mm_nt(a, b):
    return lax.dot_general(a, b, (((1,), (1,)), ((), ())), preferred_element_type=F32)


def mm3(a, b):
    return mm(a[0], b[0]) + (mm(a[0], b[1]) + mm(a[1], b[0]))


def mm3_nt(a, b):
    return mm_nt(a[0], b[0]) + (mm_nt(a[0], b[1]) + mm_nt(a[1], b[0]))


def one_hot(slots_row):
    held = jnp.transpose(jnp.broadcast_to(slots_row.astype(F32), (128, WAVES)))
    lane = lax.broadcasted_iota(jnp.int32, (WAVES, 128), 1).astype(F32) * 4.0
    return jnp.concatenate(
        [(held == lane + float(r)).astype(F32).astype(BF16) for r in RESIDUES], axis=1
    )


def head_kernel(
    slots_hbm, grid_hbm, traj_hbm, high_hbm, low_hbm, out_hbm,
    slots_ref, grid_ref, traj_ref, high_ref, low_ref, parts, sent, sems,
):
    slots = pltpu.make_async_copy(slots_hbm, slots_ref, sems.at[40])
    slots.start()
    inputs, tables = [], []
    for half in range(2):
        for q in range(4):
            columns, at = pl.ds(QUARTER * q + QUARTER // 2 * half, QUARTER // 2), 4 * half + q
            for k, (src, dst) in enumerate(((grid_hbm, grid_ref), (traj_hbm, traj_ref))):
                inputs.append(pltpu.make_async_copy(src.at[:, columns], dst.at[at], sems.at[2 * at + k]))
                inputs[-1].start()
        for k, (src, dst) in enumerate(((high_hbm, high_ref), (low_hbm, low_ref))):
            tables.append(pltpu.make_async_copy(src.at[half], dst.at[half], sems.at[32 + 2 * half + k]))
            tables[-1].start()
    slots.wait()
    pick = one_hot(slots_ref[...])

    def product(half, a, b, n):
        count = b - a
        both = jnp.concatenate([high_ref[half, a:b, :], low_ref[half, a:b, :]], axis=0)
        wide = mm_nt(both, parts[half, n, 0])
        return wide[:count] + wide[count:] + mm_nt(high_ref[half, a:b, :], parts[half, n, 1])

    def fetch(half):
        for copy in inputs[8 * half : 8 * half + 8]:
            copy.wait()

    def combine(half):
        for lat in range(0, 16, 2):
            for h in range(2):
                quarters = []
                for q in range(4):
                    picked = [
                        jnp.concatenate([ref[4 * half + q, 16 * n + 8 * h : 16 * n + 8 * h + 8, :] for n in (lat, lat + 1)])
                        for ref in (grid_ref, traj_ref)
                    ]
                    quarters.append(picked[0] * (1.0 + picked[1]))
                q0, q1, q2, q3 = quarters
                even, swing = q0 + q2, q1 + q3
                rows = pl.ds(128 * h + 8 * lat, 16)
                for n, part in enumerate((even + swing, even - swing, q0 - q2, q1 - q3)):
                    parts[half, n, 0, rows, :], parts[half, n, 1, rows, :] = split(part)

    def products(half):
        for copy in tables[2 * half : 2 * half + 2]:
            copy.wait()
        return [product(half, a, b, n) for n, (a, b) in enumerate(((0, 256), (256, 512), (512, 1024), (512, 1024)))]

    fetch(0)
    combine(0)
    sums = products(0)
    fetch(1)
    combine(1)
    sums = [x + y for x, y in zip(sums, products(1))]
    zero, two, u1, u2 = sums
    cosine = [zero[:128], two[:128], u1[:128] + u2[128:256], u1[256:384] - u2[384:]]
    sine = [zero[128:], two[128:], u1[128:256] - u2[:128], u1[384:] + u2[256:384]]
    sides = [split(jnp.concatenate(wave, axis=0)) for wave in (cosine, sine)]
    wide = jnp.concatenate([sides[0][0], sides[1][0], sides[0][1], sides[1][1]], axis=1)
    stores = []
    for n in range(4):
        found = mm(pick[128 * n : 128 * (n + 1)], wide)
        found = found[:, :512] + found[:, 512:]
        for c in range(2):
            for k in range(2):
                sent[pl.ds(512 * n + 2 * k + c, 128, stride=4), :] = found[:, 256 * c + 128 * k : 256 * c + 128 * (k + 1)]
        rows = pl.ds(512 * n, 512)
        stores.append(pltpu.make_async_copy(sent.at[rows], out_hbm.at[rows], sems.at[36 + n]))
        stores[-1].start()
    for copy in stores:
        copy.wait()


def prepare_kernel(slots_ref, p_ref, to_ref, from_ref, high_ref, low_ref, pick_ref, couple_ref):
    for n, ref in enumerate((to_ref, from_ref)):
        high, low = split(ref[...])
        couple_ref[n] = jnp.concatenate([high, high, low], axis=1)
    source = lax.broadcasted_iota(jnp.int32, (128, 128), 0)
    target = lax.broadcasted_iota(jnp.int32, (128, 128), 1)
    order = (source == (target % 8) * 16 + target // 8).astype(F32).astype(BF16)
    for s in range(2):
        for ref, value in zip((high_ref, low_ref), split(p_ref[s])):
            for g in range(4):
                lanes = slice(128 * g, 128 * (g + 1))
                ref[s, :, lanes] = mm(value[:, lanes], order).astype(BF16)
    pick_ref[...] = one_hot(slots_ref[...])


def swap_groups(tiles, lane):
    tiles = list(tiles)
    for bit in (1, 2, 4):
        mask = (lane & bit) != 0
        for i in range(8):
            if i & bit:
                continue
            a, b = tiles[i], tiles[i | bit]
            moved = jnp.take_along_axis(jnp.where(mask, a, b), lane ^ bit, axis=1)
            tiles[i], tiles[i | bit] = jnp.where(mask, moved, a), jnp.where(mask, b, moved)
    return tiles


def mid_kernel(
    waves_ref, rates_ref, couple_ref, y_ref, ph_hbm, pl_hbm, state_hbm,
    spectral_hbm, z_ref,
    ph_ref, pl_ref, state_ref, spectral_ref, scale_ref, folds, north, south, sems,
):
    sources, targets = (ph_hbm, pl_hbm, state_hbm), (ph_ref, pl_ref, state_ref)
    copies = [pltpu.make_async_copy(a, b, sems.at[k]) for k, (a, b) in enumerate(zip(sources, targets))]
    for copy in copies:
        copy.start()
    lane = lax.broadcasted_iota(jnp.int32, (8, 128), 1)
    mirror = lane ^ 120
    flip = lambda tile: jnp.take_along_axis(tile, mirror, axis=1)

    def fold_step(step, carry):
        v, g = step // 4, step % 4
        ahead = swap_groups([y_ref[(8 * g + i) * 4 + v] for i in range(8)], lane)
        behind = swap_groups([y_ref[(63 - 8 * g - i) * 4 + v] for i in range(8)], lane)
        for j in range(8):
            a, b = ahead[j], flip(behind[j])
            rows = pl.ds(pl.multiple_of(64 * v + 8 * j, 8), 8)
            folds[0, g, rows, :] = a + b
            folds[1, g, rows, :] = a - b
        return carry

    lax.fori_loop(0, 16, fold_step, 0, unroll=4)
    k_row = lax.broadcasted_iota(jnp.int32, (1, WAVES), 1)
    even_k = k_row % 2 == 0
    rate = jnp.broadcast_to(rates_ref[:, 0:1], (64, WAVES))
    for s in range(2):
        degree = (k_row + waves_ref[s : s + 1, :]).astype(F32)
        helm = degree * (degree + 1.0) / (WAVES * (WAVES - 1.0))
        scale_ref[s] = 1.0 / (1.0 + helm * rate)
    for copy in copies:
        copy.wait()
    totals = []
    for s in range(2):
        fold = []
        for par in range(2):
            for c in range(2):
                halves = [
                    jnp.concatenate(
                        [folds[par, g, pl.ds(4 * s + 2 * h + c, 32, stride=8), :] for g in range(4)], axis=1
                    )
                    for h in range(2)
                ]
                fold += [halves[h][8 * v : 8 * v + 8] for v in range(4) for h in range(2)]
        both = mm3_nt(split(jnp.concatenate(fold, axis=0)), (ph_ref[s], pl_ref[s]))
        valid = (k_row < WAVES - waves_ref[s : s + 1, :]).astype(F32)
        mixed = jnp.where(even_k, both[:128], both[128:])
        total = (mixed + state_ref[pl.ds(128 * s, 128), :]) * valid
        totals += [total[:64], total[64:]]
    h, l = split(jnp.concatenate(totals, axis=1))
    modes = mm(couple_ref[0], jnp.concatenate([h, l, h], axis=0))
    scales = [scale_ref[s] for s in (0, 0, 1, 1)]
    h, l = split(modes * jnp.concatenate(scales, axis=1))
    spectral = mm(couple_ref[1], jnp.concatenate([h, l, h], axis=0))
    for n in range(4):
        spectral_ref[pl.ds(64 * n, 64), :] = spectral[:, WAVES * n : WAVES * (n + 1)]
    store = pltpu.make_async_copy(spectral_ref, spectral_hbm, sems.at[3])
    store.start()
    for s in range(2):
        own = spectral_ref[128 * s : 128 * (s + 1), :]
        pair = jnp.concatenate([jnp.where(even_k, own, 0.0), jnp.where(even_k, 0.0, own)], axis=0)
        both = mm3(split(pair), (ph_ref[s], pl_ref[s]))
        for to, side in ((north, both[:128] + both[128:]), (south, both[:128] - both[128:])):
            for c in range(2):
                for v in range(4):
                    for h in range(2):
                        row, start = PITCH * (4 * s + 2 * h + c) + 8 * v, 64 * c + 16 * v + 8 * h
                        for g in range(4):
                            to[g, row : row + 8, :] = side[start : start + 8, 128 * g : 128 * (g + 1)]
    for v in range(4):
        for g in range(4):
            for side in (north, south):
                tiles = [side[g, pl.ds(v * 8 + j, 8, stride=PITCH), :] for j in range(8)]
                for i, tile in enumerate(swap_groups(tiles, lane)):
                    if side is north:
                        z_ref[(8 * g + i) * 4 + v] = tile
                    else:
                        z_ref[(63 - 8 * g - i) * 4 + v] = flip(tile)
    store.wait()


def tail_kernel(z_ref, pick_ref, high_ref, low_ref, out_hbm, block, sems):
    pick = pick_ref[...]
    natural = []
    for c in range(2):
        sides = [z_ref[pl.ds(2 * k + c, WAVES, stride=4), :] for k in range(2)]
        h, l = split(jnp.transpose(jnp.concatenate(sides, axis=1)))
        natural.append(split(mm(h, pick) + mm(l, pick)))
    part = lambda c, kind: tuple(natural[c][n][:, 128 * kind : 128 * (kind + 1)] for n in range(2))
    minus = lambda pair: (-pair[0], -pair[1])
    join = lambda *parts: tuple(jnp.concatenate([p[n] for p in parts], axis=1) for n in range(2))
    whole = lambda ref, a, b: jnp.concatenate([ref[0, a:b, :], ref[1, a:b, :]], axis=1)
    table = lambda a, b: (whole(high_ref, a, b), whole(low_ref, a, b))
    zero = mm3(join(part(0, 0), part(1, 0)), table(0, 256))
    two = mm3(join(part(0, 1), part(1, 1)), table(256, 512))
    odd = table(512, 1024)
    stores = []

    def put(q, value):
        for h in range(2):
            for lat in range(16):
                row = 128 * h + 8 * lat
                block[lat, 8 * h : 8 * h + 8, QUARTER * q : QUARTER * (q + 1)] = value[row : row + 8]
        columns = pl.ds(QUARTER * q, QUARTER)
        stores.append(pltpu.make_async_copy(block.at[:, :, columns], out_hbm.at[:, :, columns], sems.at[q]))
        stores[-1].start()

    plus, less = zero + two, zero - two
    first = mm3(join(part(0, 2), part(1, 2), part(0, 3), part(1, 3)), odd)
    put(0, plus + first)
    put(2, plus - first)
    turned = mm3(join(minus(part(1, 2)), part(0, 2), part(1, 3), minus(part(0, 3))), odd)
    put(1, less + turned)
    put(3, less - turned)
    for copy in stores:
        copy.wait()


VMEM = pl.BlockSpec(memory_space=pltpu.VMEM)
HBM = pl.BlockSpec(memory_space=pltpu.HBM)
DMA = pltpu.SemaphoreType.DMA


def call(kernel, name, outs, in_specs, out_specs, scratch=(), flops=0, moved=0, room=32):
    return pl.pallas_call(
        kernel,
        name=name,
        out_shape=outs,
        in_specs=in_specs,
        out_specs=out_specs,
        scratch_shapes=list(scratch),
        compiler_params=pltpu.CompilerParams(vmem_limit_bytes=room * 2**20),
        cost_estimate=pl.CostEstimate(flops=flops, bytes_accessed=moved, transcendentals=0),
    )


def shards(grid_adjoint, trajectory, legendre_north, slot_wavenumber, spectral_state, to_modes, from_modes, rates):
    shape = jax.ShapeDtypeStruct
    high, low = wave_rows()
    high, low = jnp.asarray(high), jnp.asarray(low)
    slots_row = slot_wavenumber.reshape(1, WAVES)
    device = lax.axis_index("band") * lax.axis_size("lev") + lax.axis_index("lev")
    own_waves = lax.dynamic_slice_in_dim(slot_wavenumber, 2 * device, 2)

    square = (256, LON)
    sent = call(
        head_kernel, "head", shape((2048, 128), F32), [HBM] * 5, HBM,
        [pltpu.VMEM((1, WAVES), jnp.int32)] + [pltpu.VMEM((8, 256, QUARTER // 2), F32)] * 2 + [pltpu.VMEM((2, 1024, QUARTER // 2), BF16)] * 2
        + [pltpu.VMEM((2, 4, 2, 256, QUARTER // 2), BF16), pltpu.VMEM((2048, 128), F32), DMA((41,))],
        flops=2 * 10**9, moved=7 * 10**6, room=60,
    )(slots_row, grid_adjoint.reshape(square), trajectory.reshape(square), high, low)
    arrived = lax.all_to_all(sent.reshape(256, 8, 128), ("band", "lev"), 0, 0, tiled=True)

    ph, plo, pick, couple = call(
        prepare_kernel, "prepare",
        [shape((2, 512, 512), BF16)] * 2 + [shape((512, 512), BF16), shape((2, 64, 192), BF16)],
        [VMEM] * 4, [VMEM] * 4, flops=10**8, moved=8 * 10**6,
    )(slots_row, legendre_north, to_modes, from_modes)
    state = jnp.transpose(spectral_state, (0, 2, 3, 1)).reshape(256, WAVES)
    columns = jnp.broadcast_to(rates[:, None], (64, 128))
    far = [pltpu.with_memory_space_constraint(v, pltpu.HBM) for v in (ph, plo, state)]

    legendre, rows = pltpu.VMEM((2, 512, 512), BF16), pltpu.VMEM((256, WAVES), F32)
    spectral, back = call(
        mid_kernel, "mid", [shape((256, WAVES), F32), shape((256, 8, 128), F32)],
        [VMEM] * 4 + [HBM] * 3, [HBM, VMEM],
        [legendre, legendre, rows, rows, pltpu.VMEM((2, 64, WAVES), F32), pltpu.VMEM((2, 4, 256, 128), F32)]
        + [pltpu.VMEM((4, 8 * PITCH, 128), F32)] * 2 + [DMA((4,))],
        flops=3 * 10**9, moved=8 * 10**6, room=32,
    )(jnp.broadcast_to(own_waves[:, None], (2, WAVES)), columns, couple, arrived, *far)
    returned = lax.all_to_all(back, ("band", "lev"), 0, 0, tiled=True)
    grid = call(
        tail_kernel, "tail", shape((16, 16, LON), F32), [VMEM] * 4, HBM,
        [pltpu.VMEM((16, 16, LON), F32), DMA((4,))],
        flops=2 * 10**9, moved=6 * 10**6,
    )(returned.reshape(2048, 128), pick, high, low)
    spectral_out = jnp.transpose(spectral.reshape(2, 2, 64, WAVES), (0, 3, 1, 2))
    return spectral_out, grid


def solution(mesh):
    spread = P(("band", "lev"), None, None)
    return jax.shard_map(
        shards,
        mesh=mesh,
        in_specs=(
            P("band", "lev", None), P("band", "lev", None), spread, P(),
            P(("band", "lev"), None, None, None), P(), P(), P(),
        ),
        out_specs=(P(("band", "lev"), None, None, None), P("band", "lev", None)),
        check_vma=False,
    )
```

```python
import jax
import jax.numpy as jnp
import numpy as np
from jax import lax
from jax.experimental import pallas as pl
from jax.experimental.pallas import tpu as pltpu
from jax.sharding import PartitionSpec as P

WAVES = 512
LON = 2048
QUARTER = LON // 4
RESIDUES = (0, 2, 1, 3)
PITCH = 40
BF16 = jnp.bfloat16
F32 = jnp.float32


def wave_rows():
    j = np.arange(QUARTER, dtype=np.int64)
    blocks = []
    for residue in RESIDUES:
        m = 4 * np.arange(WAVES // 4, dtype=np.int64) + residue
        angle = (m[:, None] * j[None, :] % LON) * (2.0 * np.pi / LON)
        blocks += [np.cos(angle), -np.sin(angle)]
    table = (np.concatenate(blocks, axis=0) * LON**-0.5).astype(np.float32)
    table = np.stack([table[:, : QUARTER // 2], table[:, QUARTER // 2 :]])
    high = table.astype(jnp.bfloat16)
    low = (table - high.astype(np.float32)).astype(jnp.bfloat16)
    return high, low


def split(value):
    high = value.astype(BF16)
    low = (value - high.astype(F32)).astype(BF16)
    return high, low


def mm(a, b):
    return lax.dot_general(a, b, (((1,), (0,)), ((), ())), preferred_element_type=F32)


def mm_nt(a, b):
    return lax.dot_general(a, b, (((1,), (1,)), ((), ())), preferred_element_type=F32)


def mm3(a, b):
    return mm(a[0], b[0]) + (mm(a[0], b[1]) + mm(a[1], b[0]))


def mm3_nt(a, b):
    return mm_nt(a[0], b[0]) + (mm_nt(a[0], b[1]) + mm_nt(a[1], b[0]))


def one_hot(slots_row):
    held = jnp.transpose(jnp.broadcast_to(slots_row.astype(F32), (128, WAVES)))
    lane = lax.broadcasted_iota(jnp.int32, (WAVES, 128), 1).astype(F32) * 4.0
    return jnp.concatenate(
        [(held == lane + float(r)).astype(F32).astype(BF16) for r in RESIDUES], axis=1
    )


def south_mask():
    return jnp.where(lax.axis_index("band") >= lax.axis_size("band") // 2, 15, 0)


def head_kernel(
    slots_hbm, grid_hbm, traj_hbm, high_hbm, low_hbm, out_hbm,
    slots_ref, grid_ref, traj_ref, high_ref, low_ref, parts, sent, sems,
):
    slots = pltpu.make_async_copy(slots_hbm, slots_ref, sems.at[40])
    slots.start()
    inputs, tables = [], []
    for half in range(2):
        for q in range(4):
            columns, at = pl.ds(QUARTER * q + QUARTER // 2 * half, QUARTER // 2), 4 * half + q
            for k, (src, dst) in enumerate(((grid_hbm, grid_ref), (traj_hbm, traj_ref))):
                inputs.append(pltpu.make_async_copy(src.at[:, columns], dst.at[at], sems.at[2 * at + k]))
                inputs[-1].start()
        for k, (src, dst) in enumerate(((high_hbm, high_ref), (low_hbm, low_ref))):
            tables.append(pltpu.make_async_copy(src.at[half], dst.at[half], sems.at[32 + 2 * half + k]))
            tables[-1].start()
    slots.wait()
    pick = one_hot(slots_ref[...])

    def product(half, a, b, n):
        count = b - a
        both = jnp.concatenate([high_ref[half, a:b, :], low_ref[half, a:b, :]], axis=0)
        wide = mm_nt(both, parts[half, n, 0])
        return wide[:count] + wide[count:] + mm_nt(high_ref[half, a:b, :], parts[half, n, 1])

    def fetch(half):
        for copy in inputs[8 * half : 8 * half + 8]:
            copy.wait()

    reverse = south_mask()
    level_rows = lambda lat, h: pl.ds(pl.multiple_of(16 * (lat ^ reverse) + 8 * h, 8), 8)

    def combine(half):
        for lat in range(0, 16, 2):
            for h in range(2):
                quarters = []
                for q in range(4):
                    picked = [
                        jnp.concatenate([ref[4 * half + q, level_rows(n, h), :] for n in (lat, lat + 1)])
                        for ref in (grid_ref, traj_ref)
                    ]
                    quarters.append(picked[0] * (1.0 + picked[1]))
                q0, q1, q2, q3 = quarters
                even, swing = q0 + q2, q1 + q3
                rows = pl.ds(128 * h + 8 * lat, 16)
                for n, part in enumerate((even + swing, even - swing, q0 - q2, q1 - q3)):
                    parts[half, n, 0, rows, :], parts[half, n, 1, rows, :] = split(part)

    def products(half):
        for copy in tables[2 * half : 2 * half + 2]:
            copy.wait()
        return [product(half, a, b, n) for n, (a, b) in enumerate(((0, 256), (256, 512), (512, 1024), (512, 1024)))]

    fetch(0)
    combine(0)
    sums = products(0)
    fetch(1)
    combine(1)
    sums = [x + y for x, y in zip(sums, products(1))]
    zero, two, u1, u2 = sums
    cosine = [zero[:128], two[:128], u1[:128] + u2[128:256], u1[256:384] - u2[384:]]
    sine = [zero[128:], two[128:], u1[128:256] - u2[:128], u1[384:] + u2[256:384]]
    sides = [split(jnp.concatenate(wave, axis=0)) for wave in (cosine, sine)]
    wide = jnp.concatenate([sides[0][0], sides[1][0], sides[0][1], sides[1][1]], axis=1)
    stores = []
    for n in range(4):
        found = mm(pick[128 * n : 128 * (n + 1)], wide)
        found = found[:, :512] + found[:, 512:]
        for c in range(2):
            for k in range(2):
                sent[pl.ds(512 * n + 2 * k + c, 128, stride=4), :] = found[:, 256 * c + 128 * k : 256 * c + 128 * (k + 1)]
        rows = pl.ds(512 * n, 512)
        stores.append(pltpu.make_async_copy(sent.at[rows], out_hbm.at[rows], sems.at[36 + n]))
        stores[-1].start()
    for copy in stores:
        copy.wait()


def prepare_kernel(slots_ref, p_ref, to_ref, from_ref, high_ref, low_ref, pick_ref, couple_ref):
    for n, ref in enumerate((to_ref, from_ref)):
        high, low = split(ref[...])
        couple_ref[n] = jnp.concatenate([high, high, low], axis=1)
    source = lax.broadcasted_iota(jnp.int32, (128, 128), 0)
    target = lax.broadcasted_iota(jnp.int32, (128, 128), 1)
    order = (source == (target % 8) * 16 + target // 8).astype(F32).astype(BF16)
    for s in range(2):
        for ref, value in zip((high_ref, low_ref), split(p_ref[s])):
            for g in range(4):
                lanes = slice(128 * g, 128 * (g + 1))
                ref[s, :, lanes] = mm(value[:, lanes], order).astype(BF16)
    pick_ref[...] = one_hot(slots_ref[...])


def swap_groups(tiles, lane):
    tiles = list(tiles)
    for bit in (1, 2, 4):
        mask = (lane & bit) != 0
        for i in range(8):
            if i & bit:
                continue
            a, b = tiles[i], tiles[i | bit]
            moved = jnp.take_along_axis(jnp.where(mask, a, b), lane ^ bit, axis=1)
            tiles[i], tiles[i | bit] = jnp.where(mask, moved, a), jnp.where(mask, b, moved)
    return tiles


def mid_kernel(
    waves_ref, rates_ref, couple_ref, y_ref, ph_hbm, pl_hbm, state_hbm,
    spectral_hbm, z_ref,
    ph_ref, pl_ref, state_ref, spectral_ref, scale_ref, folds, north, south, sems,
):
    copies = []
    for s in range(2):
        rows = pl.ds(128 * s, 128)
        pairs = ((ph_hbm.at[s], ph_ref.at[s]), (pl_hbm.at[s], pl_ref.at[s]), (state_hbm.at[rows], state_ref.at[rows]))
        copies.append([pltpu.make_async_copy(a, b, sems.at[3 * s + k]) for k, (a, b) in enumerate(pairs)])
        for copy in copies[s]:
            copy.start()
    lane = lax.broadcasted_iota(jnp.int32, (8, 128), 1)

    def fold_step(step, carry):
        v, g = step // 4, step % 4
        ahead = swap_groups([y_ref[(8 * g + i) * 4 + v] for i in range(8)], lane)
        behind = swap_groups([y_ref[(63 - 8 * g - i) * 4 + v] for i in range(8)], lane)
        for j in range(8):
            a, b = ahead[j], behind[j]
            rows = pl.ds(pl.multiple_of(64 * v + 8 * j, 8), 8)
            folds[0, g, rows, :] = a + b
            folds[1, g, rows, :] = a - b
        return carry

    lax.fori_loop(0, 16, fold_step, 0, unroll=4)
    k_row = lax.broadcasted_iota(jnp.int32, (1, WAVES), 1)
    even_k = k_row % 2 == 0
    rate = jnp.broadcast_to(rates_ref[:, 0:1], (64, WAVES))
    for s in range(2):
        degree = (k_row + waves_ref[s : s + 1, :]).astype(F32)
        helm = degree * (degree + 1.0) / (WAVES * (WAVES - 1.0))
        scale_ref[s] = 1.0 / (1.0 + helm * rate)
    totals = []
    for s in range(2):
        for copy in copies[s]:
            copy.wait()
        fold = []
        for par in range(2):
            for c in range(2):
                halves = [
                    jnp.concatenate(
                        [folds[par, g, pl.ds(4 * s + 2 * h + c, 32, stride=8), :] for g in range(4)], axis=1
                    )
                    for h in range(2)
                ]
                fold += [halves[h][8 * v : 8 * v + 8] for v in range(4) for h in range(2)]
        both = mm3_nt(split(jnp.concatenate(fold, axis=0)), (ph_ref[s], pl_ref[s]))
        valid = (k_row < WAVES - waves_ref[s : s + 1, :]).astype(F32)
        mixed = jnp.where(even_k, both[:128], both[128:])
        total = (mixed + state_ref[pl.ds(128 * s, 128), :]) * valid
        totals += [total[:64], total[64:]]
    h, l = split(jnp.concatenate(totals, axis=1))
    modes = mm(couple_ref[0], jnp.concatenate([h, l, h], axis=0))
    scales = [scale_ref[s] for s in (0, 0, 1, 1)]
    h, l = split(modes * jnp.concatenate(scales, axis=1))
    spectral = mm(couple_ref[1], jnp.concatenate([h, l, h], axis=0))
    for n in range(4):
        spectral_ref[pl.ds(64 * n, 64), :] = spectral[:, WAVES * n : WAVES * (n + 1)]
    store = pltpu.make_async_copy(spectral_ref, spectral_hbm, sems.at[6])
    store.start()
    for s in range(2):
        own = spectral_ref[128 * s : 128 * (s + 1), :]
        pair = jnp.concatenate([jnp.where(even_k, own, 0.0), jnp.where(even_k, 0.0, own)], axis=0)
        both = mm3(split(pair), (ph_ref[s], pl_ref[s]))
        for to, side in ((north, both[:128] + both[128:]), (south, both[:128] - both[128:])):
            for c in range(2):
                for v in range(4):
                    for h in range(2):
                        row, start = PITCH * (4 * s + 2 * h + c) + 8 * v, 64 * c + 16 * v + 8 * h
                        for g in range(4):
                            to[g, row : row + 8, :] = side[start : start + 8, 128 * g : 128 * (g + 1)]
    for v in range(4):
        for g in range(4):
            for side in (north, south):
                tiles = [side[g, pl.ds(v * 8 + j, 8, stride=PITCH), :] for j in range(8)]
                for i, tile in enumerate(swap_groups(tiles, lane)):
                    if side is north:
                        z_ref[(8 * g + i) * 4 + v] = tile
                    else:
                        z_ref[(63 - 8 * g - i) * 4 + v] = tile
    store.wait()


def tail_kernel(z_ref, pick_ref, high_ref, low_ref, out_hbm, block, sems):
    pick = pick_ref[...]
    natural = []
    for c in range(2):
        sides = [z_ref[pl.ds(2 * k + c, WAVES, stride=4), :] for k in range(2)]
        h, l = split(jnp.transpose(jnp.concatenate(sides, axis=1)))
        natural.append(split(mm(h, pick) + mm(l, pick)))
    part = lambda c, kind: tuple(natural[c][n][:, 128 * kind : 128 * (kind + 1)] for n in range(2))
    minus = lambda pair: (-pair[0], -pair[1])
    join = lambda *parts: tuple(jnp.concatenate([p[n] for p in parts], axis=1) for n in range(2))
    whole = lambda ref, a, b: jnp.concatenate([ref[0, a:b, :], ref[1, a:b, :]], axis=1)
    table = lambda a, b: (whole(high_ref, a, b), whole(low_ref, a, b))
    zero = mm3(join(part(0, 0), part(1, 0)), table(0, 256))
    two = mm3(join(part(0, 1), part(1, 1)), table(256, 512))
    odd = table(512, 1024)
    stores = []
    reverse = south_mask()

    def put(q, value):
        for h in range(2):
            for lat in range(16):
                row = 128 * h + 8 * lat
                block[lat ^ reverse, 8 * h : 8 * h + 8, QUARTER * q : QUARTER * (q + 1)] = value[row : row + 8]
        columns = pl.ds(QUARTER * q, QUARTER)
        stores.append(pltpu.make_async_copy(block.at[:, :, columns], out_hbm.at[:, :, columns], sems.at[q]))
        stores[-1].start()

    plus, less = zero + two, zero - two
    first = mm3(join(part(0, 2), part(1, 2), part(0, 3), part(1, 3)), odd)
    put(0, plus + first)
    put(2, plus - first)
    turned = mm3(join(minus(part(1, 2)), part(0, 2), part(1, 3), minus(part(0, 3))), odd)
    put(1, less + turned)
    put(3, less - turned)
    for copy in stores:
        copy.wait()


VMEM = pl.BlockSpec(memory_space=pltpu.VMEM)
HBM = pl.BlockSpec(memory_space=pltpu.HBM)
DMA = pltpu.SemaphoreType.DMA


def call(kernel, name, outs, in_specs, out_specs, scratch=(), flops=0, moved=0, room=32):
    return pl.pallas_call(
        kernel,
        name=name,
        out_shape=outs,
        in_specs=in_specs,
        out_specs=out_specs,
        scratch_shapes=list(scratch),
        compiler_params=pltpu.CompilerParams(vmem_limit_bytes=room * 2**20),
        cost_estimate=pl.CostEstimate(flops=flops, bytes_accessed=moved, transcendentals=0),
    )


def shards(grid_adjoint, trajectory, legendre_north, slot_wavenumber, spectral_state, to_modes, from_modes, rates):
    shape = jax.ShapeDtypeStruct
    high, low = wave_rows()
    high, low = jnp.asarray(high), jnp.asarray(low)
    slots_row = slot_wavenumber.reshape(1, WAVES)
    device = lax.axis_index("band") * lax.axis_size("lev") + lax.axis_index("lev")
    own_waves = lax.dynamic_slice_in_dim(slot_wavenumber, 2 * device, 2)

    square = (256, LON)
    sent = call(
        head_kernel, "head", shape((2048, 128), F32), [HBM] * 5, HBM,
        [pltpu.VMEM((1, WAVES), jnp.int32)] + [pltpu.VMEM((8, 256, QUARTER // 2), F32)] * 2 + [pltpu.VMEM((2, 1024, QUARTER // 2), BF16)] * 2
        + [pltpu.VMEM((2, 4, 2, 256, QUARTER // 2), BF16), pltpu.VMEM((2048, 128), F32), DMA((41,))],
        flops=2 * 10**9, moved=7 * 10**6, room=60,
    )(slots_row, grid_adjoint.reshape(square), trajectory.reshape(square), high, low)
    arrived = lax.all_to_all(sent.reshape(256, 8, 128), ("band", "lev"), 0, 0, tiled=True)

    ph, plo, pick, couple = call(
        prepare_kernel, "prepare",
        [shape((2, 512, 512), BF16)] * 2 + [shape((512, 512), BF16), shape((2, 64, 192), BF16)],
        [VMEM] * 4, [VMEM] * 4, flops=10**8, moved=8 * 10**6,
    )(slots_row, legendre_north, to_modes, from_modes)
    state = jnp.transpose(spectral_state, (0, 2, 3, 1)).reshape(256, WAVES)
    columns = jnp.broadcast_to(rates[:, None], (64, 128))
    far = [pltpu.with_memory_space_constraint(v, pltpu.HBM) for v in (ph, plo, state)]

    legendre, rows = pltpu.VMEM((2, 512, 512), BF16), pltpu.VMEM((256, WAVES), F32)
    spectral, back = call(
        mid_kernel, "mid", [shape((256, WAVES), F32), shape((256, 8, 128), F32)],
        [VMEM] * 4 + [HBM] * 3, [HBM, VMEM],
        [legendre, legendre, rows, rows, pltpu.VMEM((2, 64, WAVES), F32), pltpu.VMEM((2, 4, 256, 128), F32)]
        + [pltpu.VMEM((4, 8 * PITCH, 128), F32)] * 2 + [DMA((7,))],
        flops=3 * 10**9, moved=8 * 10**6, room=32,
    )(jnp.broadcast_to(own_waves[:, None], (2, WAVES)), columns, couple, arrived, *far)
    returned = lax.all_to_all(back, ("band", "lev"), 0, 0, tiled=True)
    grid = call(
        tail_kernel, "tail", shape((16, 16, LON), F32), [VMEM] * 4, HBM,
        [pltpu.VMEM((16, 16, LON), F32), DMA((4,))],
        flops=2 * 10**9, moved=6 * 10**6,
    )(returned.reshape(2048, 128), pick, high, low)
    spectral_out = jnp.transpose(spectral.reshape(2, 2, 64, WAVES), (0, 3, 1, 2))
    return spectral_out, grid


def solution(mesh):
    spread = P(("band", "lev"), None, None)
    return jax.shard_map(
        shards,
        mesh=mesh,
        in_specs=(
            P("band", "lev", None), P("band", "lev", None), spread, P(),
            P(("band", "lev"), None, None, None), P(), P(), P(),
        ),
        out_specs=(P(("band", "lev"), None, None, None), P("band", "lev", None)),
        check_vma=False,
    )
```

```python
import jax
import jax.numpy as jnp
import numpy as np
from jax import lax
from jax.experimental import pallas as pl
from jax.experimental.pallas import tpu as pltpu
from jax.sharding import PartitionSpec as P

WAVES = 512
LON = 2048
QUARTER = LON // 4
RESIDUES = (0, 2, 1, 3)
PITCH = 40
BF16 = jnp.bfloat16
F32 = jnp.float32


def wave_rows():
    j = np.arange(QUARTER, dtype=np.int64)
    blocks = []
    for residue in RESIDUES:
        m = 4 * np.arange(WAVES // 4, dtype=np.int64) + residue
        angle = (m[:, None] * j[None, :] % LON) * (2.0 * np.pi / LON)
        blocks += [np.cos(angle), -np.sin(angle)]
    table = (np.concatenate(blocks, axis=0) * LON**-0.5).astype(np.float32)
    table = np.stack([table[:, : QUARTER // 2], table[:, QUARTER // 2 :]])
    high = table.astype(jnp.bfloat16)
    low = (table - high.astype(np.float32)).astype(jnp.bfloat16)
    return high, low


def split(value):
    high = value.astype(BF16)
    low = (value - high.astype(F32)).astype(BF16)
    return high, low


def mm(a, b):
    return lax.dot_general(a, b, (((1,), (0,)), ((), ())), preferred_element_type=F32)


def mm_nt(a, b):
    return lax.dot_general(a, b, (((1,), (1,)), ((), ())), preferred_element_type=F32)


def mm3(a, b):
    return mm(jnp.concatenate([a[0], a[0], a[1]], axis=1), jnp.concatenate([b[0], b[1], b[0]], axis=0))


def mm3_nt(a, b):
    return mm_nt(a[0], b[0]) + (mm_nt(a[0], b[1]) + mm_nt(a[1], b[0]))


def one_hot(slots_row):
    held = jnp.transpose(jnp.broadcast_to(slots_row.astype(F32), (128, WAVES)))
    lane = lax.broadcasted_iota(jnp.int32, (WAVES, 128), 1).astype(F32) * 4.0
    return jnp.concatenate(
        [(held == lane + float(r)).astype(F32).astype(BF16) for r in RESIDUES], axis=1
    )


def south_mask():
    return jnp.where(lax.axis_index("band") >= lax.axis_size("band") // 2, 15, 0)


def head_kernel(
    slots_hbm, grid_hbm, traj_hbm, high_hbm, low_hbm, out_hbm,
    slots_ref, grid_ref, traj_ref, high_ref, low_ref, parts, sent, sems,
):
    slots = pltpu.make_async_copy(slots_hbm, slots_ref, sems.at[40])
    slots.start()
    inputs, tables = [], []
    for half in range(2):
        for q in range(4):
            columns, at = pl.ds(QUARTER * q + QUARTER // 2 * half, QUARTER // 2), 4 * half + q
            for k, (src, dst) in enumerate(((grid_hbm, grid_ref), (traj_hbm, traj_ref))):
                inputs.append(pltpu.make_async_copy(src.at[:, columns], dst.at[at], sems.at[2 * at + k]))
                inputs[-1].start()
        for k, (src, dst) in enumerate(((high_hbm, high_ref), (low_hbm, low_ref))):
            tables.append(pltpu.make_async_copy(src.at[half], dst.at[half], sems.at[32 + 2 * half + k]))
            tables[-1].start()
    slots.wait()
    pick = one_hot(slots_ref[...])

    def product(half, a, b, n):
        count = b - a
        both = jnp.concatenate([high_ref[half, a:b, :], low_ref[half, a:b, :]], axis=0)
        wide = mm_nt(both, parts[half, n, 0])
        return wide[:count] + wide[count:] + mm_nt(high_ref[half, a:b, :], parts[half, n, 1])

    def fetch(half):
        for copy in inputs[8 * half : 8 * half + 8]:
            copy.wait()

    reverse = south_mask()
    level_rows = lambda lat, h: pl.ds(pl.multiple_of(16 * (lat ^ reverse) + 8 * h, 8), 8)

    def combine(half):
        for lat in range(0, 16, 2):
            for h in range(2):
                quarters = []
                for q in range(4):
                    picked = [
                        jnp.concatenate([ref[4 * half + q, level_rows(n, h), :] for n in (lat, lat + 1)])
                        for ref in (grid_ref, traj_ref)
                    ]
                    quarters.append(picked[0] * (1.0 + picked[1]))
                q0, q1, q2, q3 = quarters
                even, swing = q0 + q2, q1 + q3
                rows = pl.ds(128 * h + 8 * lat, 16)
                for n, part in enumerate((even + swing, even - swing, q0 - q2, q1 - q3)):
                    parts[half, n, 0, rows, :], parts[half, n, 1, rows, :] = split(part)

    def products(half):
        for copy in tables[2 * half : 2 * half + 2]:
            copy.wait()
        return [product(half, a, b, n) for n, (a, b) in enumerate(((0, 256), (256, 512), (512, 1024), (512, 1024)))]

    fetch(0)
    combine(0)
    sums = products(0)
    fetch(1)
    combine(1)
    sums = [x + y for x, y in zip(sums, products(1))]
    zero, two, u1, u2 = sums
    cosine = [zero[:128], two[:128], u1[:128] + u2[128:256], u1[256:384] - u2[384:]]
    sine = [zero[128:], two[128:], u1[128:256] - u2[:128], u1[384:] + u2[256:384]]
    sides = [split(jnp.concatenate(wave, axis=0)) for wave in (cosine, sine)]
    wide = jnp.concatenate([sides[0][0], sides[1][0], sides[0][1], sides[1][1]], axis=1)
    stores = []
    for n in range(4):
        found = mm(pick[128 * n : 128 * (n + 1)], wide)
        found = found[:, :512] + found[:, 512:]
        for c in range(2):
            for k in range(2):
                sent[pl.ds(512 * n + 2 * k + c, 128, stride=4), :] = found[:, 256 * c + 128 * k : 256 * c + 128 * (k + 1)]
        rows = pl.ds(512 * n, 512)
        stores.append(pltpu.make_async_copy(sent.at[rows], out_hbm.at[rows], sems.at[36 + n]))
        stores[-1].start()
    for copy in stores:
        copy.wait()


def prepare_kernel(slots_ref, p_ref, to_ref, from_ref, high_ref, low_ref, pick_ref, couple_ref):
    for n, ref in enumerate((to_ref, from_ref)):
        high, low = split(ref[...])
        couple_ref[n] = jnp.concatenate([high, high, low], axis=1)
    source = lax.broadcasted_iota(jnp.int32, (128, 128), 0)
    target = lax.broadcasted_iota(jnp.int32, (128, 128), 1)
    order = (source == (target % 8) * 16 + target // 8).astype(F32).astype(BF16)
    for s in range(2):
        for ref, value in zip((high_ref, low_ref), split(p_ref[s])):
            for g in range(4):
                lanes = slice(128 * g, 128 * (g + 1))
                ref[s, :, lanes] = mm(value[:, lanes], order).astype(BF16)
    pick_ref[...] = one_hot(slots_ref[...])


def swap_groups(tiles, lane):
    tiles = list(tiles)
    for bit in (1, 2, 4):
        mask = (lane & bit) != 0
        for i in range(8):
            if i & bit:
                continue
            a, b = tiles[i], tiles[i | bit]
            moved = jnp.take_along_axis(jnp.where(mask, a, b), lane ^ bit, axis=1)
            tiles[i], tiles[i | bit] = jnp.where(mask, moved, a), jnp.where(mask, b, moved)
    return tiles


def mid_kernel(
    waves_ref, rates_ref, couple_ref, y_ref, ph_hbm, pl_hbm, state_hbm,
    spectral_hbm, z_ref,
    ph_ref, pl_ref, state_ref, spectral_ref, scale_ref, folds, north, south, sems,
):
    copies = []
    for s in range(2):
        rows = pl.ds(128 * s, 128)
        pairs = ((ph_hbm.at[s], ph_ref.at[s]), (pl_hbm.at[s], pl_ref.at[s]), (state_hbm.at[rows], state_ref.at[rows]))
        copies.append([pltpu.make_async_copy(a, b, sems.at[3 * s + k]) for k, (a, b) in enumerate(pairs)])
        for copy in copies[s]:
            copy.start()
    lane = lax.broadcasted_iota(jnp.int32, (8, 128), 1)

    def fold_step(step, carry):
        v, g = step // 4, step % 4
        ahead = swap_groups([y_ref[(8 * g + i) * 4 + v] for i in range(8)], lane)
        behind = swap_groups([y_ref[(63 - 8 * g - i) * 4 + v] for i in range(8)], lane)
        for j in range(8):
            a, b = ahead[j], behind[j]
            rows = pl.ds(pl.multiple_of(64 * v + 8 * j, 8), 8)
            folds[0, g, rows, :] = a + b
            folds[1, g, rows, :] = a - b
        return carry

    lax.fori_loop(0, 16, fold_step, 0, unroll=4)
    k_row = lax.broadcasted_iota(jnp.int32, (1, WAVES), 1)
    even_k = k_row % 2 == 0
    rate = jnp.broadcast_to(rates_ref[:, 0:1], (64, WAVES))
    for s in range(2):
        degree = (k_row + waves_ref[s : s + 1, :]).astype(F32)
        helm = degree * (degree + 1.0) / (WAVES * (WAVES - 1.0))
        scale_ref[s] = 1.0 / (1.0 + helm * rate)
    totals = []
    for s in range(2):
        for copy in copies[s]:
            copy.wait()
        fold = []
        for par in range(2):
            for c in range(2):
                halves = [
                    jnp.concatenate(
                        [folds[par, g, pl.ds(4 * s + 2 * h + c, 32, stride=8), :] for g in range(4)], axis=1
                    )
                    for h in range(2)
                ]
                fold += [halves[h][8 * v : 8 * v + 8] for v in range(4) for h in range(2)]
        both = mm3_nt(split(jnp.concatenate(fold, axis=0)), (ph_ref[s], pl_ref[s]))
        valid = (k_row < WAVES - waves_ref[s : s + 1, :]).astype(F32)
        mixed = jnp.where(even_k, both[:128], both[128:])
        total = (mixed + state_ref[pl.ds(128 * s, 128), :]) * valid
        totals += [total[:64], total[64:]]
    h, l = split(jnp.concatenate(totals, axis=1))
    modes = mm(couple_ref[0], jnp.concatenate([h, l, h], axis=0))
    scales = [scale_ref[s] for s in (0, 0, 1, 1)]
    h, l = split(modes * jnp.concatenate(scales, axis=1))
    spectral = mm(couple_ref[1], jnp.concatenate([h, l, h], axis=0))
    for n in range(4):
        spectral_ref[pl.ds(64 * n, 64), :] = spectral[:, WAVES * n : WAVES * (n + 1)]
    store = pltpu.make_async_copy(spectral_ref, spectral_hbm, sems.at[6])
    store.start()
    for s in range(2):
        own = spectral_ref[128 * s : 128 * (s + 1), :]
        pair = jnp.concatenate([jnp.where(even_k, own, 0.0), jnp.where(even_k, 0.0, own)], axis=0)
        both = mm3(split(pair), (ph_ref[s], pl_ref[s]))
        for to, side in ((north, both[:128] + both[128:]), (south, both[:128] - both[128:])):
            for c in range(2):
                for v in range(4):
                    for h in range(2):
                        row, start = PITCH * (4 * s + 2 * h + c) + 8 * v, 64 * c + 16 * v + 8 * h
                        for g in range(4):
                            to[g, row : row + 8, :] = side[start : start + 8, 128 * g : 128 * (g + 1)]
    for v in range(4):
        for g in range(4):
            for side in (north, south):
                tiles = [side[g, pl.ds(v * 8 + j, 8, stride=PITCH), :] for j in range(8)]
                for i, tile in enumerate(swap_groups(tiles, lane)):
                    if side is north:
                        z_ref[(8 * g + i) * 4 + v] = tile
                    else:
                        z_ref[(63 - 8 * g - i) * 4 + v] = tile
    store.wait()


def tail_kernel(z_ref, pick_ref, high_ref, low_ref, out_hbm, block, sems):
    pick = pick_ref[...]
    natural = []
    for c in range(2):
        sides = [z_ref[pl.ds(2 * k + c, WAVES, stride=4), :] for k in range(2)]
        h, l = split(jnp.transpose(jnp.concatenate(sides, axis=1)))
        natural.append(split(mm(h, pick) + mm(l, pick)))
    part = lambda c, kind: tuple(natural[c][n][:, 128 * kind : 128 * (kind + 1)] for n in range(2))
    minus = lambda pair: (-pair[0], -pair[1])
    join = lambda *parts: tuple(jnp.concatenate([p[n] for p in parts], axis=1) for n in range(2))
    whole = lambda ref, a, b: jnp.concatenate([ref[0, a:b, :], ref[1, a:b, :]], axis=1)
    table = lambda a, b: (whole(high_ref, a, b), whole(low_ref, a, b))
    zero = mm3(join(part(0, 0), part(1, 0)), table(0, 256))
    two = mm3(join(part(0, 1), part(1, 1)), table(256, 512))
    odd = table(512, 1024)
    stores = []
    reverse = south_mask()

    def put(q, value):
        for h in range(2):
            for lat in range(16):
                row = 128 * h + 8 * lat
                block[lat ^ reverse, 8 * h : 8 * h + 8, QUARTER * q : QUARTER * (q + 1)] = value[row : row + 8]
        columns = pl.ds(QUARTER * q, QUARTER)
        stores.append(pltpu.make_async_copy(block.at[:, :, columns], out_hbm.at[:, :, columns], sems.at[q]))
        stores[-1].start()

    plus, less = zero + two, zero - two
    first = mm3(join(part(0, 2), part(1, 2), part(0, 3), part(1, 3)), odd)
    put(0, plus + first)
    put(2, plus - first)
    turned = mm3(join(minus(part(1, 2)), part(0, 2), part(1, 3), minus(part(0, 3))), odd)
    put(1, less + turned)
    put(3, less - turned)
    for copy in stores:
        copy.wait()


VMEM = pl.BlockSpec(memory_space=pltpu.VMEM)
HBM = pl.BlockSpec(memory_space=pltpu.HBM)
DMA = pltpu.SemaphoreType.DMA


def call(kernel, name, outs, in_specs, out_specs, scratch=(), flops=0, moved=0, room=32):
    return pl.pallas_call(
        kernel,
        name=name,
        out_shape=outs,
        in_specs=in_specs,
        out_specs=out_specs,
        scratch_shapes=list(scratch),
        compiler_params=pltpu.CompilerParams(vmem_limit_bytes=room * 2**20),
        cost_estimate=pl.CostEstimate(flops=flops, bytes_accessed=moved, transcendentals=0),
    )


def shards(grid_adjoint, trajectory, legendre_north, slot_wavenumber, spectral_state, to_modes, from_modes, rates):
    shape = jax.ShapeDtypeStruct
    high, low = wave_rows()
    high, low = jnp.asarray(high), jnp.asarray(low)
    slots_row = slot_wavenumber.reshape(1, WAVES)
    device = lax.axis_index("band") * lax.axis_size("lev") + lax.axis_index("lev")
    own_waves = lax.dynamic_slice_in_dim(slot_wavenumber, 2 * device, 2)

    square = (256, LON)
    sent = call(
        head_kernel, "head", shape((2048, 128), F32), [HBM] * 5, HBM,
        [pltpu.VMEM((1, WAVES), jnp.int32)] + [pltpu.VMEM((8, 256, QUARTER // 2), F32)] * 2 + [pltpu.VMEM((2, 1024, QUARTER // 2), BF16)] * 2
        + [pltpu.VMEM((2, 4, 2, 256, QUARTER // 2), BF16), pltpu.VMEM((2048, 128), F32), DMA((41,))],
        flops=2 * 10**9, moved=7 * 10**6, room=60,
    )(slots_row, grid_adjoint.reshape(square), trajectory.reshape(square), high, low)
    arrived = lax.all_to_all(sent.reshape(256, 8, 128), ("band", "lev"), 0, 0, tiled=True)

    ph, plo, pick, couple = call(
        prepare_kernel, "prepare",
        [shape((2, 512, 512), BF16)] * 2 + [shape((512, 512), BF16), shape((2, 64, 192), BF16)],
        [VMEM] * 4, [VMEM] * 4, flops=10**8, moved=8 * 10**6,
    )(slots_row, legendre_north, to_modes, from_modes)
    state = jnp.transpose(spectral_state, (0, 2, 3, 1)).reshape(256, WAVES)
    columns = jnp.broadcast_to(rates[:, None], (64, 128))
    far = [pltpu.with_memory_space_constraint(v, pltpu.HBM) for v in (ph, plo, state)]

    legendre, rows = pltpu.VMEM((2, 512, 512), BF16), pltpu.VMEM((256, WAVES), F32)
    spectral, back = call(
        mid_kernel, "mid", [shape((256, WAVES), F32), shape((256, 8, 128), F32)],
        [VMEM] * 4 + [HBM] * 3, [HBM, VMEM],
        [legendre, legendre, rows, rows, pltpu.VMEM((2, 64, WAVES), F32), pltpu.VMEM((2, 4, 256, 128), F32)]
        + [pltpu.VMEM((4, 8 * PITCH, 128), F32)] * 2 + [DMA((7,))],
        flops=3 * 10**9, moved=8 * 10**6, room=32,
    )(jnp.broadcast_to(own_waves[:, None], (2, WAVES)), columns, couple, arrived, *far)
    returned = lax.all_to_all(back, ("band", "lev"), 0, 0, tiled=True)
    grid = call(
        tail_kernel, "tail", shape((16, 16, LON), F32), [VMEM] * 4, HBM,
        [pltpu.VMEM((16, 16, LON), F32), DMA((4,))],
        flops=2 * 10**9, moved=6 * 10**6,
    )(returned.reshape(2048, 128), pick, high, low)
    spectral_out = jnp.transpose(spectral.reshape(2, 2, 64, WAVES), (0, 3, 1, 2))
    return spectral_out, grid


def solution(mesh):
    spread = P(("band", "lev"), None, None)
    return jax.shard_map(
        shards,
        mesh=mesh,
        in_specs=(
            P("band", "lev", None), P("band", "lev", None), spread, P(),
            P(("band", "lev"), None, None, None), P(), P(), P(),
        ),
        out_specs=(P(("band", "lev"), None, None, None), P("band", "lev", None)),
        check_vma=False,
    )
```
